32 devices in a mesh: grp: 4 (over y, x), tp: 8 (over z, core).
Axes of the slice: x: 2, y: 2, z: 4, core: 2. Of those that a mesh axis runs over, the one named last changes fastest.
Arguments:
- batch_sizes: int32 [4], P('grp'), may hold values from 1 to 16
- seq_lens: int32 [4, 16], P('grp'), may hold values from 1 to 2048
- page_table: int32 [4, 16, 128], P('grp', None, 'tp'), may hold values from 0 to 255, as said below
- queries: bfloat16 [4, 16, 4096], P('grp', None, 'tp'), may hold values from -4 to 14
- kv_pool: bfloat16 [4, 2048, 16, 1024], P('grp', 'tp'), may hold values from -7 to 7
- new_kv: bfloat16 [4, 16, 1024], P('grp'), may hold values from -6 to 6
- out_weight: bfloat16 [4096, 2880], P('tp', 'grp'), may hold values from -0.375 to 0.375
Outputs:
- mixed: float32 [4, 16, 2880], P('grp')
The draws below stay inside these ranges and needn't reach their ends.
Inputs may be any that keep to these rules, and one draw needn't show every extreme that they name: `batch_sizes`: slots below a group's batch size are live; the others are empty and their outputs are zero. `seq_lens`: entries of empty slots are drawn but unused. `page_table`: for every group g and every t, the entries [g, :, t * 16 to (t + 1) * 16 - 1] are a permutation of 0 to 255.
All inputs are finite; a program needn't handle non-finite values.
Results may differ from the reference program's by a relative error of at most 0.007.
Values may be sent and summed in bfloat16 or wider, within the bound.
A program may use at most 64 MiB of HBM per device.

```python
import jax
import jax.numpy as jnp
from jax import lax

D = 2880
HEADS = 64
KV_HEADS = 8
HD = 64
PAGE = 16
PAGES_DEV = 16
SLOTS = 16
GROUPS = 4
POOL_DEV = 256
MAX_LEN = 2048
N_TP = 8


def draw_page_table(key, part):
    subkeys = jax.random.split(jax.random.fold_in(key, 101), GROUPS * N_TP)
    orders = jax.vmap(lambda single: jax.random.permutation(single, POOL_DEV))(subkeys)
    orders = orders.reshape(GROUPS, N_TP, SLOTS, PAGES_DEV).transpose(0, 2, 1, 3)
    return orders.reshape(GROUPS, SLOTS, N_TP * PAGES_DEV).astype(jnp.int32)


def draw_queries(key, part):
    noise = jax.random.normal(jax.random.fold_in(key, 11), (GROUPS, SLOTS, HEADS * HD), jnp.float32)
    noise = jnp.clip(noise, -4.0, 4.0)
    return noise.astype(jnp.bfloat16)


def draw_kv_pool(key, part):
    extent = (GROUPS, N_TP * POOL_DEV, PAGE, 2 * KV_HEADS * HD)
    column = jnp.arange(2 * KV_HEADS * HD)
    key_column = column < KV_HEADS * HD
    noise = jnp.clip(jax.random.normal(jax.random.fold_in(key, 22), extent, jnp.float32), -4.0, 4.0)
    noise = noise * jnp.where(key_column, 1.5, 1.0)
    return noise.astype(jnp.bfloat16)


def set_ends(values, rng, smallest, top_value):
    spot = [jax.random.randint(jax.random.fold_in(rng, axis), (), 0, length) for axis, length in enumerate(values.shape)]
    main_axis = values.shape.index(max(values.shape))
    beside = spot[:main_axis] + [(spot[main_axis] + 1) % values.shape[main_axis]] + spot[main_axis + 1:]
    return values.at[tuple(spot)].set(smallest).at[tuple(beside)].set(top_value)


def block_levels(key, shape, cuts, low, top_value):
    def one(dim, shards_of):
        draws = jax.random.uniform(jax.random.fold_in(jax.random.fold_in(key, 6), dim), (shards_of,), jnp.float32, low / len(cuts), top_value / len(cuts))
        return jnp.repeat(jnp.exp(draws), shape[dim] // shards_of).reshape((-1,) + (1,) * (len(shape) - dim - 1))

    factor_of = one(*cuts[0])
    for cut in cuts[1:]:
        factor_of = factor_of * one(*cut)
    return factor_of


def scatter_about(rng, dims, spread, bound, pieces=(), kind=jnp.bfloat16):
    values = jax.random.normal(rng, dims, jnp.float32) * spread
    if len(pieces) > 0:
        values = block_levels(rng, dims, pieces, -0.22, 0.18) * values
    return jnp.clip(values, min=-bound, max=bound).astype(kind)


def setup_inputs(seed: int = 0) -> dict:
    streams_of = jax.random.split(jax.random.key(seed), 8)
    batch_sizes = set_ends(jax.random.randint(streams_of[0], (GROUPS,), 1, SLOTS + 1), jax.random.fold_in(streams_of[0], 1), 1, SLOTS).astype(jnp.int32)
    seq_lens = set_ends(jax.random.randint(streams_of[1], (GROUPS, SLOTS), 1, MAX_LEN + 1), jax.random.fold_in(streams_of[1], 1), 1, MAX_LEN).astype(jnp.int32)
    page_table = draw_page_table(jax.random.fold_in(streams_of[7], 71), 0)
    queries = draw_queries(jax.random.fold_in(streams_of[7], 71), 0)
    kv_pool = draw_kv_pool(jax.random.fold_in(streams_of[7], 71), 0)
    new_kv = scatter_about(streams_of[5], (GROUPS, SLOTS, 2 * KV_HEADS * HD), 1.0, 6.0, ((0, 4),))
    out_weight = scatter_about(streams_of[6], (HEADS * HD, D), (HEADS * HD // 16) ** -0.5, 0.375, ((0, 8), (1, 4)))
    return dict(batch_sizes=batch_sizes, seq_lens=seq_lens, page_table=page_table, queries=queries, kv_pool=kv_pool, new_kv=new_kv, out_weight=out_weight)


PRECISE = lax.Precision.HIGHEST
NEG_BIG = -1.0e30


def slot_output(query_row, length, entries, group_pool, fresh_row):
    entry_ids = jnp.arange(N_TP * PAGES_DEV, dtype=jnp.int32)
    owner_dev = entry_ids // PAGES_DEV
    within = entry_ids % PAGES_DEV
    pool_rows = owner_dev * POOL_DEV + entries.astype(jnp.int32)
    page_number = within * N_TP + owner_dev
    position = (page_number[:, None] * PAGE + jnp.arange(PAGE, dtype=jnp.int32)[None, :]).reshape(-1)
    tokens = group_pool[pool_rows].reshape(N_TP * PAGES_DEV * PAGE, 2 * KV_HEADS * HD).astype(jnp.float32)
    keys_all = tokens[:, : KV_HEADS * HD].reshape(-1, KV_HEADS, HD)
    values_all = tokens[:, KV_HEADS * HD:].reshape(-1, KV_HEADS, HD)
    grouped = query_row.astype(jnp.float32).reshape(KV_HEADS, HEADS // KV_HEADS, HD)
    score_scale = HD ** -0.5
    scores = jnp.einsum("kgd,tkd->kgt", grouped, keys_all, precision=PRECISE) * score_scale
    valid_mask = (position < length)[None, None, :]
    scores = jnp.where(valid_mask, scores, NEG_BIG)
    fresh = fresh_row.astype(jnp.float32)
    new_key = fresh[: KV_HEADS * HD].reshape(KV_HEADS, HD)
    new_value = fresh[KV_HEADS * HD:].reshape(KV_HEADS, HD)
    own_score = jnp.einsum("kgd,kd->kg", grouped, new_key, precision=PRECISE) * score_scale
    top_score = jnp.maximum(jnp.max(scores, axis=2), own_score)
    weights = jnp.where(valid_mask, jnp.exp(scores - top_score[:, :, None]), 0.0)
    rounded = lax.optimization_barrier(weights.astype(jnp.bfloat16)).astype(jnp.float32)
    own_weight = jnp.exp(own_score - top_score)
    numerator = jnp.einsum("kgt,tkd->kgd", rounded, values_all, precision=PRECISE)
    numerator = numerator + own_weight[:, :, None] * new_value[:, None, :]
    denominator = jnp.sum(weights, axis=2) + own_weight
    return (numerator / denominator[:, :, None]).reshape(HEADS * HD)


def group_output(inputs):
    live_count, lengths, page_ids, group_queries, group_pool, group_new = inputs

    def one_slot(slot_item):
        query_row, length, entries, fresh_row = slot_item
        return slot_output(query_row, length, entries, group_pool, fresh_row)

    slot_rows = lax.map(one_slot, (group_queries, lengths, page_ids, group_new))
    live_mask = jnp.arange(SLOTS, dtype=jnp.int32) < live_count
    return jnp.where(live_mask[:, None], slot_rows, 0.0).astype(jnp.bfloat16)


def reference(batch_sizes, seq_lens, page_table, queries, kv_pool, new_kv, out_weight):
    attended = lax.map(group_output, (batch_sizes, seq_lens, page_table, queries, kv_pool, new_kv))
    flat_rows = attended.reshape(GROUPS * SLOTS, HEADS * HD)
    mixed = jnp.dot(flat_rows, out_weight, preferred_element_type=jnp.float32)
    return mixed.reshape(GROUPS, SLOTS, D).astype(jnp.float32)
```

```python
import functools

import jax
import jax.numpy as jnp
from jax import lax
from jax.experimental import pallas as pl
from jax.experimental.pallas import tpu as pltpu
from jax.sharding import PartitionSpec as P

HD = 64
LANES = 128
NEG_BIG = -1e30
POOL_CHUNKS = 8
MESH = pl.DeviceIdType.MESH


def fused_kernel(
    cfg,
    bs_ref,
    len_ref,
    pt_ref,
    q_hbm,
    kv_hbm,
    nkv_ref,
    w_hbm,
    out_ref,
    kv_v,
    w_v,
    q_all,
    q_bd,
    wbuf,
    w_send,
    st_send,
    w_recv,
    st_recv,
    att_all,
    ps,
    rs,
    red,
    og,
    local_sem,
    q_ssem,
    q_rsem,
    w_ssem,
    w_rsem,
    st_ssem,
    st_rsem,
    a_ssem,
    a_rsem,
    p_ssem,
    p_rsem,
    o_ssem,
    o_rsem,
):
    tp, grp, heads, kv_heads, slots, pages, page_len, cols, per, share = cfg
    t = lax.axis_index("tp")
    j = lax.axis_index("grp")
    group_size = heads // kv_heads
    own = heads // tp
    half_slots = slots // 2
    half_kv = kv_heads // 2
    tokens = pages * page_len
    key_width = kv_heads * HD
    win = key_width // 2
    owner_grp = lax.div(t, share)
    self_part = owner_grp == j

    def tp_peer(d):
        return lax.rem(t + d, tp)

    def tp_src(d):
        return lax.rem(t + (tp - d), tp)

    pool_pages = kv_v.shape[0]
    step = pool_pages // POOL_CHUNKS
    local = [
        pltpu.make_async_copy(
            kv_hbm.at[0, pl.ds(i * step, step)],
            kv_v.at[pl.ds(i * step, step)],
            local_sem.at[i],
        )
        for i in range(POOL_CHUNKS)
    ]
    w_copy = pltpu.make_async_copy(w_hbm, w_v, local_sem.at[POOL_CHUNKS])
    q_copy = pltpu.make_async_copy(q_hbm.at[0], q_all.at[t], local_sem.at[POOL_CHUNKS + 1])
    q_copy.start()
    for copy in local:
        copy.start()
    w_copy.start()

    barrier = pltpu.get_barrier_semaphore()
    for d in range(1, tp):
        pl.semaphore_signal(barrier, inc=1, device_id=(j, tp_peer(d)), device_id_type=MESH)
    for a in range(1, grp):
        pl.semaphore_signal(
            barrier, inc=1, device_id=(lax.rem(j + a, grp), t), device_id_type=MESH
        )
    for d in range(tp):
        src_t = tp_peer(d)
        if d == 0:

            @pl.when(jnp.logical_not(self_part))
            def _():
                pl.semaphore_signal(
                    barrier, inc=1, device_id=(owner_grp, src_t), device_id_type=MESH
                )

        else:
            pl.semaphore_signal(barrier, inc=1, device_id=(owner_grp, src_t), device_id_type=MESH)

    q_bd[...] = jnp.zeros_like(q_bd)
    ps[...] = jnp.zeros_like(ps)
    arrivals = (tp - 1) + (grp - 1) + grp * share
    pl.semaphore_wait(barrier, arrivals - self_part.astype(jnp.int32))

    q_sends = []
    for d in range(1, tp):
        copy = pltpu.make_async_remote_copy(
            src_ref=q_hbm.at[0],
            dst_ref=q_all.at[t],
            send_sem=q_ssem.at[d],
            recv_sem=q_rsem.at[t],
            device_id=(j, tp_peer(d)),
            device_id_type=MESH,
        )
        copy.start()
        q_sends.append(copy)
    q_copy.wait()

    lane = lax.broadcasted_iota(jnp.int32, (half_slots, LANES), 1)
    low = lane < HD

    kv_own = lax.div(t * own, group_size)
    odd = lax.rem(kv_own, 2)
    lane2 = lax.broadcasted_iota(jnp.int32, (slots, LANES), 1)
    low2 = lane2 < HD

    def kv_tile(base):
        start = pl.multiple_of(base + lax.div(kv_own, 2) * LANES, LANES)
        x = nkv_ref[0, :, pl.ds(start, LANES)].astype(jnp.float32)
        flipped = pltpu.roll(x, HD, 1)
        flip = jnp.broadcast_to(odd, x.shape) == 1
        first = jnp.where(flip, flipped, x)
        return jnp.where(low2, first, pltpu.roll(first, HD, 1))

    new_key = kv_tile(0)
    new_val = kv_tile(key_width)
    val_packed = jnp.where(low, new_val[:half_slots], new_val[half_slots:])
    q_own = q_all[t].astype(jnp.float32)
    prod = q_own * jnp.concatenate([new_key] * (own // 2), axis=1)
    prod_hi = prod.astype(jnp.bfloat16)
    prod_lo = (prod - prod_hi.astype(jnp.float32)).astype(jnp.bfloat16)
    e_row = lax.broadcasted_iota(jnp.int32, (own * HD, LANES), 0) // HD
    e_col = lax.broadcasted_iota(jnp.int32, (own * HD, LANES), 1) % own
    spread = jnp.where(e_row == e_col, 1.0, 0.0).astype(jnp.bfloat16)
    self_score = jnp.dot(prod_hi, spread, preferred_element_type=jnp.float32) + jnp.dot(
        prod_lo, spread, preferred_element_type=jnp.float32
    )
    self_score = self_score * (HD**-0.5)

    for d in range(1, tp):
        src = tp_src(d)
        pltpu.make_async_remote_copy(
            src_ref=q_hbm.at[0],
            dst_ref=q_all.at[src],
            send_sem=q_ssem.at[d],
            recv_sem=q_rsem.at[src],
            device_id=(j, src),
            device_id_type=MESH,
        ).wait_recv()
    for src in range(tp):
        rows = q_all[src].astype(jnp.float32) * (HD**-0.5)
        for pair in range(own // 2):
            tile = rows[:, pair * LANES : (pair + 1) * LANES]
            turned = pltpu.roll(tile, HD, 1)
            for side in range(2):
                head = src * own + pair * 2 + side
                kv = head // group_size
                value = tile if side == kv % 2 else turned
                keep = low2 if kv % 2 == 0 else jnp.logical_not(low2)
                value = jnp.where(keep, value, 0.0)
                q_bd[
                    (kv % half_kv) // 2, pl.ds(head, slots, stride=heads), :
                ] = value

    for copy in local:
        copy.wait()

    col = lax.broadcasted_iota(jnp.int32, (heads, tokens), 1)
    position = ((col // page_len) * tp + t) * page_len + col % page_len
    stat_lane = lax.broadcasted_iota(jnp.int32, (heads, LANES), 1)
    win_lane = lax.broadcasted_iota(jnp.int32, (group_size, win), 1) // HD
    tiles_in_win = win // LANES
    rows_in_win = half_kv * group_size

    def one_slot(s, stats):
        first = pl.multiple_of(s * heads, heads)
        ids = [pt_ref[0, s, i] for i in range(pages)]
        length = len_ref[0, s]

        def block(start):
            return jnp.concatenate(
                [kv_v[ids[i], :, start : start + win] for i in range(pages)], axis=0
            )

        scores = []
        for w in range(2):
            q_w = jnp.concatenate(
                [
                    q_bd[k, pl.ds(first + w * rows_in_win, rows_in_win), :]
                    for k in range(tiles_in_win)
                ],
                axis=1,
            ).astype(jnp.bfloat16)
            scores.append(
                lax.dot_general(
                    q_w,
                    block(w * win),
                    (((1,), (1,)), ((), ())),
                    preferred_element_type=jnp.float32,
                )
            )
        scores = jnp.concatenate(scores, axis=0)
        valid = position < length
        scores = jnp.where(valid, scores, NEG_BIG)
        top = jnp.max(scores, axis=1, keepdims=True)
        weights = jnp.where(valid, jnp.exp(scores - top), 0.0)
        total = jnp.sum(weights, axis=1, keepdims=True)
        rounded = weights.astype(jnp.bfloat16)
        tiles = []
        for w in range(2):
            o = jnp.dot(
                rounded[w * rows_in_win : (w + 1) * rows_in_win],
                block(key_width + w * win),
                preferred_element_type=jnp.float32,
            )
            folded = jnp.zeros((group_size, win), jnp.float32)
            for k in range(half_kv):
                folded = jnp.where(
                    win_lane == k, o[k * group_size : (k + 1) * group_size], folded
                )
            for k in range(tiles_in_win):
                tiles.append(folded[:, k * LANES : (k + 1) * LANES])
        stats = jnp.where(stat_lane == s, top, stats)
        stats = jnp.where(stat_lane == s + slots, total, stats)
        return tiles, stats

    g_low = lax.broadcasted_iota(jnp.int32, (group_size, LANES), 1) < HD

    def slot_pair(s, stats):
        tiles_a, stats = one_slot(s, stats)
        tiles_b, stats = one_slot(s + half_slots, stats)
        for k in range(kv_heads // 2):
            even = jnp.where(g_low, tiles_a[k], pltpu.roll(tiles_b[k], HD, 1))
            odd_t = jnp.where(g_low, pltpu.roll(tiles_a[k], HD, 1), tiles_b[k])
            span = group_size * half_slots
            wbuf[pl.ds(2 * k * span + s, group_size, stride=half_slots), :] = even
            wbuf[pl.ds((2 * k + 1) * span + s, group_size, stride=half_slots), :] = odd_t
        return stats

    stats = lax.fori_loop(0, half_slots, slot_pair, jnp.zeros((heads, LANES), jnp.float32))

    for dst in range(tp):
        span = own * half_slots
        w_send[dst] = wbuf[dst * span : (dst + 1) * span, :].astype(jnp.bfloat16)
        st_send[dst] = stats[dst * own : (dst + 1) * own]

    part_sends = []
    for d in range(1, tp):
        peer = tp_peer(d)
        for src_buf, dst_buf, ssem, rsem in (
            (st_send, st_recv, st_ssem, st_rsem),
            (w_send, w_recv, w_ssem, w_rsem),
        ):
            copy = pltpu.make_async_remote_copy(
                src_ref=src_buf.at[peer],
                dst_ref=dst_buf.at[t],
                send_sem=ssem.at[d],
                recv_sem=rsem.at[t],
                device_id=(j, peer),
                device_id_type=MESH,
            )
            copy.start()
            part_sends.append(copy)
    w_recv[t] = w_send[t]
    st_recv[t] = st_send[t]
    w_copy.wait()
    for d in range(1, tp):
        src = tp_src(d)
        pltpu.make_async_remote_copy(
            src_ref=st_send.at[src],
            dst_ref=st_recv.at[src],
            send_sem=st_ssem.at[d],
            recv_sem=st_rsem.at[src],
            device_id=(j, src),
            device_id_type=MESH,
        ).wait_recv()
    stacked = jnp.concatenate([st_recv[src] for src in range(tp)] * (LANES // heads), axis=0)
    turned = jnp.transpose(stacked)
    hs = half_slots

    def across(x, op):
        shift = own
        while shift < heads:
            x = op(x, pltpu.roll(x, shift, 1))
            shift *= 2
        return x

    parts, selfs = [], []
    for h in range(2):
        top = turned[h * hs : (h + 1) * hs]
        total = turned[slots + h * hs : slots + (h + 1) * hs]
        self_h = self_score[h * hs : (h + 1) * hs]
        final = jnp.maximum(across(top, jnp.maximum), self_h)
        scale = jnp.exp(top - final)
        self_w = jnp.exp(self_h - final)
        denominator = across(scale * total, jnp.add) + self_w
        parts.append(scale / denominator)
        selfs.append(self_w / denominator)

    def half_cast(pieces, c):
        return jnp.where(
            low,
            jnp.broadcast_to(pieces[0][:, c : c + 1], (hs, LANES)),
            jnp.broadcast_to(pieces[1][:, c : c + 1], (hs, LANES)),
        )

    sums = [half_cast(selfs, g) * val_packed for g in range(own)]
    for d in range(1, tp):
        src = tp_src(d)
        pltpu.make_async_remote_copy(
            src_ref=w_send.at[src],
            dst_ref=w_recv.at[src],
            send_sem=w_ssem.at[d],
            recv_sem=w_rsem.at[src],
            device_id=(j, src),
            device_id_type=MESH,
        ).wait_recv()
    for src in range(tp):
        block = w_recv[src].astype(jnp.float32)
        for g in range(own):
            sums[g] = sums[g] + half_cast(parts, src * own + g) * block[g * hs : (g + 1) * hs]
    tiles = []
    for k in range(own // 2):
        a, b = sums[2 * k], sums[2 * k + 1]
        upper = jnp.where(low, a, pltpu.roll(b, HD, 1))
        lower = jnp.where(low, pltpu.roll(a, HD, 1), b)
        tiles.append(jnp.concatenate([upper, lower], axis=0))
    attended = jnp.concatenate(tiles, axis=1)
    slot_row = lax.broadcasted_iota(jnp.int32, attended.shape, 0)
    attended = jnp.where(slot_row < bs_ref[0], attended, 0.0).astype(jnp.bfloat16)
    att_all[j] = attended

    a_sends = []
    for a in range(1, grp):
        copy = pltpu.make_async_remote_copy(
            src_ref=att_all.at[j],
            dst_ref=att_all.at[j],
            send_sem=a_ssem.at[a],
            recv_sem=a_rsem.at[j],
            device_id=(lax.rem(j + a, grp), t),
            device_id_type=MESH,
        )
        copy.start()
        a_sends.append(copy)
    for a in range(1, grp):
        src = lax.rem(j + (grp - a), grp)
        pltpu.make_async_remote_copy(
            src_ref=att_all.at[src],
            dst_ref=att_all.at[src],
            send_sem=a_ssem.at[a],
            recv_sem=a_rsem.at[src],
            device_id=(src, t),
            device_id_type=MESH,
        ).wait_recv()
    lhs = jnp.concatenate([att_all[g] for g in range(grp)], axis=0)
    projected = jnp.dot(lhs, w_v[...], preferred_element_type=jnp.float32)
    width = per * LANES
    for g in range(grp):
        for k in range(share):
            lo, hi = k * width, min((k + 1) * width, cols)
            if lo < hi:
                ps[g, k, :, 0 : hi - lo] = projected[g * slots : (g + 1) * slots, lo:hi].astype(
                    jnp.bfloat16
                )

    p_sends = []
    for a in range(grp):
        dst_g = lax.rem(j + a, grp)
        for k in range(share):
            dst_t = share * j + k
            copy = pltpu.make_async_remote_copy(
                src_ref=ps.at[dst_g, k],
                dst_ref=rs.at[t],
                send_sem=p_ssem.at[a, k],
                recv_sem=p_rsem.at[t],
                device_id=(dst_g, dst_t),
                device_id_type=MESH,
            )
            if a == 0:
                here = dst_t == t

                @pl.when(jnp.logical_not(here))
                def _():
                    copy.start()

                @pl.when(here)
                def _():
                    rs[t] = ps[j, k]

                p_sends.append((copy, here))
            else:
                copy.start()
                p_sends.append((copy, None))
    for d in range(tp):
        src = tp_src(d)
        copy = pltpu.make_async_remote_copy(
            src_ref=ps.at[0, 0],
            dst_ref=rs.at[src],
            send_sem=p_ssem.at[0, 0],
            recv_sem=p_rsem.at[src],
            device_id=(owner_grp, src),
            device_id_type=MESH,
        )
        if d == 0:

            @pl.when(jnp.logical_not(self_part))
            def _():
                copy.wait_recv()

        else:
            copy.wait_recv()
    total = rs[0].astype(jnp.float32)
    for src in range(1, tp):
        total = total + rs[src].astype(jnp.float32)
    red[...] = total.astype(jnp.bfloat16)

    o_sends = []
    for d in range(1, tp):
        copy = pltpu.make_async_remote_copy(
            src_ref=red,
            dst_ref=og.at[t],
            send_sem=o_ssem.at[d],
            recv_sem=o_rsem.at[t],
            device_id=(j, tp_peer(d)),
            device_id_type=MESH,
        )
        copy.start()
        o_sends.append(copy)
    og[t] = red[...]
    for copy in q_sends + part_sends + a_sends:
        copy.wait_send()
    for copy, here in p_sends:
        if here is None:
            copy.wait_send()
        else:

            @pl.when(jnp.logical_not(here))
            def _():
                copy.wait_send()

    for d in range(1, tp):
        src = tp_src(d)
        pltpu.make_async_remote_copy(
            src_ref=red,
            dst_ref=og.at[src],
            send_sem=o_ssem.at[d],
            recv_sem=o_rsem.at[src],
            device_id=(j, src),
            device_id_type=MESH,
        ).wait_recv()
    pieces = []
    for g in range(grp):
        for k in range(share):
            size = min((k + 1) * width, cols) - k * width
            if size > 0:
                pieces.append(og[g * share + k][:, :size].astype(jnp.float32))
    out_ref[0] = jnp.concatenate(pieces, axis=1)
    for copy in o_sends:
        copy.wait_send()


def local(tp, grp, batch_sizes, seq_lens, page_table, queries, kv_pool, new_kv, out_weight):
    slots, pages = page_table.shape[1:]
    pool_pages, page_len, row_width = kv_pool.shape[1:]
    kv_heads = row_width // (2 * HD)
    own_width = queries.shape[2]
    own = own_width // HD
    heads = own * tp
    rows, cols = out_weight.shape
    share = tp // grp
    tiles = -(-cols // LANES)
    per = -(-tiles // share)
    half = slots // 2
    cfg = (tp, grp, heads, kv_heads, slots, pages, page_len, cols, per, share)
    bf16, f32 = jnp.bfloat16, jnp.float32
    sem = pltpu.SemaphoreType.DMA
    vmem, smem, hbm = (
        pl.BlockSpec(memory_space=pltpu.VMEM),
        pl.BlockSpec(memory_space=pltpu.SMEM),
        pl.BlockSpec(memory_space=pl.ANY),
    )
    return pl.pallas_call(
        functools.partial(fused_kernel, cfg),
        out_shape=jax.ShapeDtypeStruct((1, slots, cols * grp), f32),
        in_specs=[smem, smem, smem, hbm, hbm, vmem, hbm],
        out_specs=vmem,
        scratch_shapes=[
            pltpu.VMEM((pool_pages, page_len, row_width), bf16),
            pltpu.VMEM((rows, cols), bf16),
            pltpu.VMEM((tp, slots, own_width), bf16),
            pltpu.VMEM((kv_heads * HD // (2 * LANES), slots * heads, LANES), f32),
            pltpu.VMEM((heads * half, LANES), f32),
            pltpu.VMEM((tp, own * half, LANES), bf16),
            pltpu.VMEM((tp, own, LANES), f32),
            pltpu.VMEM((tp, own * half, LANES), bf16),
            pltpu.VMEM((tp, own, LANES), f32),
            pltpu.VMEM((grp, slots, own_width), bf16),
            pltpu.VMEM((grp, share, slots, per * LANES), bf16),
            pltpu.VMEM((tp, slots, per * LANES), bf16),
            pltpu.VMEM((slots, per * LANES), bf16),
            pltpu.VMEM((tp, slots, per * LANES), bf16),
            sem((POOL_CHUNKS + 2,)),
            sem((tp,)),
            sem((tp,)),
            sem((tp,)),
            sem((tp,)),
            sem((tp,)),
            sem((tp,)),
            sem((grp,)),
            sem((grp,)),
            sem((grp, share)),
            sem((tp,)),
            sem((tp,)),
            sem((tp,)),
        ],
        compiler_params=pltpu.CompilerParams(
            collective_id=0, has_side_effects=True, vmem_limit_bytes=40 * 1024 * 1024
        ),
        name="fused_decode",
    )(batch_sizes, seq_lens, page_table, queries, kv_pool, new_kv, out_weight)


def solution(mesh):
    return jax.shard_map(
        functools.partial(local, mesh.shape["tp"], mesh.shape["grp"]),
        mesh=mesh,
        in_specs=(
            P("grp"),
            P("grp", None),
            P("grp", None, "tp"),
            P("grp", None, "tp"),
            P("grp", "tp", None, None),
            P("grp", None, None),
            P("tp", "grp"),
        ),
        out_specs=P("grp", None, None),
        check_vma=False,
    )
```

```python
import functools

import jax
import jax.numpy as jnp
from jax import lax
from jax.experimental import pallas as pl
from jax.experimental.pallas import tpu as pltpu
from jax.sharding import PartitionSpec as P

HD = 64
LANES = 128
NEG_BIG = -1e30
POOL_CHUNKS = 8
MESH = pl.DeviceIdType.MESH


def fused_kernel(
    cfg,
    bs_ref,
    len_hbm,
    pt_hbm,
    q_hbm,
    kv_hbm,
    nkv_hbm,
    w_hbm,
    out_ref,
    len_ref,
    pt_ref,
    nkv_ref,
    kv_v,
    w_v,
    q_all,
    q_bd,
    wbuf,
    w_send,
    st_send,
    w_recv,
    st_recv,
    att_all,
    ps,
    rs,
    red,
    og,
    local_sem,
    q_ssem,
    q_rsem,
    w_ssem,
    w_rsem,
    st_ssem,
    st_rsem,
    a_ssem,
    a_rsem,
    p_ssem,
    p_rsem,
    o_ssem,
    o_rsem,
):
    tp, grp, heads, kv_heads, slots, pages, page_len, cols, per, share = cfg
    t = lax.axis_index("tp")
    j = lax.axis_index("grp")
    group_size = heads // kv_heads
    own = heads // tp
    half_slots = slots // 2
    half_kv = kv_heads // 2
    tokens = pages * page_len
    key_width = kv_heads * HD
    win = key_width // 2
    owner_grp = lax.div(t, share)
    self_part = owner_grp == j

    def tp_peer(d):
        return lax.rem(t + d, tp)

    def tp_src(d):
        return lax.rem(t + (tp - d), tp)

    pool_pages = kv_v.shape[0]
    step = pool_pages // POOL_CHUNKS
    local = [
        pltpu.make_async_copy(
            kv_hbm.at[0, pl.ds(i * step, step)],
            kv_v.at[pl.ds(i * step, step)],
            local_sem.at[i],
        )
        for i in range(POOL_CHUNKS)
    ]
    w_copy = pltpu.make_async_copy(w_hbm, w_v, local_sem.at[POOL_CHUNKS])
    q_copy = pltpu.make_async_copy(q_hbm.at[0], q_all.at[t], local_sem.at[POOL_CHUNKS + 1])
    nkv_copy = pltpu.make_async_copy(nkv_hbm, nkv_ref, local_sem.at[POOL_CHUNKS + 2])
    len_copy = pltpu.make_async_copy(len_hbm, len_ref, local_sem.at[POOL_CHUNKS + 3])
    pt_copy = pltpu.make_async_copy(pt_hbm, pt_ref, local_sem.at[POOL_CHUNKS + 4])
    q_copy.start()
    nkv_copy.start()
    len_copy.start()
    pt_copy.start()
    for copy in local:
        copy.start()
    w_copy.start()

    barrier = pltpu.get_barrier_semaphore()
    for d in range(1, tp):
        pl.semaphore_signal(barrier, inc=1, device_id=(j, tp_peer(d)), device_id_type=MESH)
    for a in range(1, grp):
        pl.semaphore_signal(
            barrier, inc=1, device_id=(lax.rem(j + a, grp), t), device_id_type=MESH
        )
    q_bd[...] = jnp.zeros_like(q_bd)
    ps[...] = jnp.zeros_like(ps)
    pl.semaphore_wait(barrier, (tp - 1) + (grp - 1))

    q_sends = []
    for d in range(1, tp):
        copy = pltpu.make_async_remote_copy(
            src_ref=q_hbm.at[0],
            dst_ref=q_all.at[t],
            send_sem=q_ssem.at[d],
            recv_sem=q_rsem.at[t],
            device_id=(j, tp_peer(d)),
            device_id_type=MESH,
        )
        copy.start()
        q_sends.append(copy)
    q_copy.wait()
    nkv_copy.wait()

    lane = lax.broadcasted_iota(jnp.int32, (half_slots, LANES), 1)
    low = lane < HD

    kv_own = lax.div(t * own, group_size)
    odd = lax.rem(kv_own, 2)
    lane2 = lax.broadcasted_iota(jnp.int32, (slots, LANES), 1)
    low2 = lane2 < HD

    def kv_tile(base):
        start = pl.multiple_of(base + lax.div(kv_own, 2) * LANES, LANES)
        x = nkv_ref[0, :, pl.ds(start, LANES)].astype(jnp.float32)
        flipped = pltpu.roll(x, HD, 1)
        flip = jnp.broadcast_to(odd, x.shape) == 1
        first = jnp.where(flip, flipped, x)
        return jnp.where(low2, first, pltpu.roll(first, HD, 1))

    new_key = kv_tile(0)
    new_val = kv_tile(key_width)
    val_packed = jnp.where(low, new_val[:half_slots], new_val[half_slots:])
    q_own = q_all[t].astype(jnp.float32)
    prod = q_own * jnp.concatenate([new_key] * (own // 2), axis=1)
    prod_hi = prod.astype(jnp.bfloat16)
    prod_lo = (prod - prod_hi.astype(jnp.float32)).astype(jnp.bfloat16)
    e_row = lax.broadcasted_iota(jnp.int32, (own * HD, LANES), 0) // HD
    e_col = lax.broadcasted_iota(jnp.int32, (own * HD, LANES), 1) % own
    spread = jnp.where(e_row == e_col, 1.0, 0.0).astype(jnp.bfloat16)
    self_score = jnp.dot(prod_hi, spread, preferred_element_type=jnp.float32) + jnp.dot(
        prod_lo, spread, preferred_element_type=jnp.float32
    )
    self_score = self_score * (HD**-0.5)

    for d in range(1, tp):
        src = tp_src(d)
        pltpu.make_async_remote_copy(
            src_ref=q_hbm.at[0],
            dst_ref=q_all.at[src],
            send_sem=q_ssem.at[d],
            recv_sem=q_rsem.at[src],
            device_id=(j, src),
            device_id_type=MESH,
        ).wait_recv()
    for src in range(tp):
        rows = q_all[src].astype(jnp.float32) * (HD**-0.5)
        for pair in range(own // 2):
            tile = rows[:, pair * LANES : (pair + 1) * LANES]
            turned = pltpu.roll(tile, HD, 1)
            for side in range(2):
                head = src * own + pair * 2 + side
                kv = head // group_size
                value = tile if side == kv % 2 else turned
                keep = low2 if kv % 2 == 0 else jnp.logical_not(low2)
                value = jnp.where(keep, value, 0.0)
                q_bd[
                    (kv % half_kv) // 2, pl.ds(head, slots, stride=heads), :
                ] = value

    len_copy.wait()
    pt_copy.wait()
    for copy in local:
        copy.wait()

    col = lax.broadcasted_iota(jnp.int32, (heads, tokens), 1)
    position = ((col // page_len) * tp + t) * page_len + col % page_len
    stat_lane = lax.broadcasted_iota(jnp.int32, (heads, LANES), 1)
    win_lane = lax.broadcasted_iota(jnp.int32, (group_size, win), 1) // HD
    tiles_in_win = win // LANES
    rows_in_win = half_kv * group_size

    def one_slot(s, stats):
        first = pl.multiple_of(s * heads, heads)
        ids = [pt_ref[0, s, i] for i in range(pages)]
        length = len_ref[0, s]

        def block(start):
            return jnp.concatenate(
                [kv_v[ids[i], :, start : start + win] for i in range(pages)], axis=0
            )

        scores = []
        for w in range(2):
            q_w = jnp.concatenate(
                [
                    q_bd[k, pl.ds(first + w * rows_in_win, rows_in_win), :]
                    for k in range(tiles_in_win)
                ],
                axis=1,
            ).astype(jnp.bfloat16)
            scores.append(
                lax.dot_general(
                    q_w,
                    block(w * win),
                    (((1,), (1,)), ((), ())),
                    preferred_element_type=jnp.float32,
                )
            )
        scores = jnp.concatenate(scores, axis=0)
        valid = position < length
        scores = jnp.where(valid, scores, NEG_BIG)
        top = jnp.max(scores, axis=1, keepdims=True)
        weights = jnp.where(valid, jnp.exp(scores - top), 0.0)
        total = jnp.sum(weights, axis=1, keepdims=True)
        rounded = weights.astype(jnp.bfloat16)
        tiles = []
        for w in range(2):
            o = jnp.dot(
                rounded[w * rows_in_win : (w + 1) * rows_in_win],
                block(key_width + w * win),
                preferred_element_type=jnp.float32,
            )
            folded = jnp.zeros((group_size, win), jnp.float32)
            for k in range(half_kv):
                folded = jnp.where(
                    win_lane == k, o[k * group_size : (k + 1) * group_size], folded
                )
            for k in range(tiles_in_win):
                tiles.append(folded[:, k * LANES : (k + 1) * LANES])
        stats = jnp.where(stat_lane == s, top, stats)
        stats = jnp.where(stat_lane == s + slots, total, stats)
        return tiles, stats

    g_low = lax.broadcasted_iota(jnp.int32, (group_size, LANES), 1) < HD

    def slot_pair(s, stats):
        tiles_a, stats = one_slot(s, stats)
        tiles_b, stats = one_slot(s + half_slots, stats)
        for k in range(kv_heads // 2):
            even = jnp.where(g_low, tiles_a[k], pltpu.roll(tiles_b[k], HD, 1))
            odd_t = jnp.where(g_low, pltpu.roll(tiles_a[k], HD, 1), tiles_b[k])
            span = group_size * half_slots
            wbuf[pl.ds(2 * k * span + s, group_size, stride=half_slots), :] = even
            wbuf[pl.ds((2 * k + 1) * span + s, group_size, stride=half_slots), :] = odd_t
        return stats

    stats = lax.fori_loop(0, half_slots, slot_pair, jnp.zeros((heads, LANES), jnp.float32))

    for dst in range(tp):
        span = own * half_slots
        w_send[dst] = wbuf[dst * span : (dst + 1) * span, :].astype(jnp.bfloat16)
        st_send[dst] = stats[dst * own : (dst + 1) * own]

    part_sends = []
    for d in range(1, tp):
        peer = tp_peer(d)
        for src_buf, dst_buf, ssem, rsem in (
            (st_send, st_recv, st_ssem, st_rsem),
            (w_send, w_recv, w_ssem, w_rsem),
        ):
            copy = pltpu.make_async_remote_copy(
                src_ref=src_buf.at[peer],
                dst_ref=dst_buf.at[t],
                send_sem=ssem.at[d],
                recv_sem=rsem.at[t],
                device_id=(j, peer),
                device_id_type=MESH,
            )
            copy.start()
            part_sends.append(copy)
    w_recv[t] = w_send[t]
    st_recv[t] = st_send[t]
    w_copy.wait()
    for d in range(1, tp):
        src = tp_src(d)
        pltpu.make_async_remote_copy(
            src_ref=st_send.at[src],
            dst_ref=st_recv.at[src],
            send_sem=st_ssem.at[d],
            recv_sem=st_rsem.at[src],
            device_id=(j, src),
            device_id_type=MESH,
        ).wait_recv()
    stacked = jnp.concatenate([st_recv[src] for src in range(tp)] * (LANES // heads), axis=0)
    turned = jnp.transpose(stacked)
    hs = half_slots

    def across(x, op):
        shift = own
        while shift < heads:
            x = op(x, pltpu.roll(x, shift, 1))
            shift *= 2
        return x

    parts, selfs = [], []
    for h in range(2):
        top = turned[h * hs : (h + 1) * hs]
        total = turned[slots + h * hs : slots + (h + 1) * hs]
        self_h = self_score[h * hs : (h + 1) * hs]
        final = jnp.maximum(across(top, jnp.maximum), self_h)
        scale = jnp.exp(top - final)
        self_w = jnp.exp(self_h - final)
        denominator = across(scale * total, jnp.add) + self_w
        parts.append(scale / denominator)
        selfs.append(self_w / denominator)

    def half_cast(pieces, c):
        return jnp.where(
            low,
            jnp.broadcast_to(pieces[0][:, c : c + 1], (hs, LANES)),
            jnp.broadcast_to(pieces[1][:, c : c + 1], (hs, LANES)),
        )

    sums = [half_cast(selfs, g) * val_packed for g in range(own)]
    for d in range(1, tp):
        src = tp_src(d)
        pltpu.make_async_remote_copy(
            src_ref=w_send.at[src],
            dst_ref=w_recv.at[src],
            send_sem=w_ssem.at[d],
            recv_sem=w_rsem.at[src],
            device_id=(j, src),
            device_id_type=MESH,
        ).wait_recv()
    for src in range(tp):
        block = w_recv[src].astype(jnp.float32)
        for g in range(own):
            sums[g] = sums[g] + half_cast(parts, src * own + g) * block[g * hs : (g + 1) * hs]
    tiles = []
    for k in range(own // 2):
        a, b = sums[2 * k], sums[2 * k + 1]
        upper = jnp.where(low, a, pltpu.roll(b, HD, 1))
        lower = jnp.where(low, pltpu.roll(a, HD, 1), b)
        tiles.append(jnp.concatenate([upper, lower], axis=0))
    attended = jnp.concatenate(tiles, axis=1)
    slot_row = lax.broadcasted_iota(jnp.int32, attended.shape, 0)
    attended = jnp.where(slot_row < bs_ref[0], attended, 0.0).astype(jnp.bfloat16)
    att_all[j] = attended

    a_sends = []
    for a in range(1, grp):
        copy = pltpu.make_async_remote_copy(
            src_ref=att_all.at[j],
            dst_ref=att_all.at[j],
            send_sem=a_ssem.at[a],
            recv_sem=a_rsem.at[j],
            device_id=(lax.rem(j + a, grp), t),
            device_id_type=MESH,
        )
        copy.start()
        a_sends.append(copy)
    for a in range(1, grp):
        src = lax.rem(j + (grp - a), grp)
        pltpu.make_async_remote_copy(
            src_ref=att_all.at[src],
            dst_ref=att_all.at[src],
            send_sem=a_ssem.at[a],
            recv_sem=a_rsem.at[src],
            device_id=(src, t),
            device_id_type=MESH,
        ).wait_recv()
    lhs = jnp.concatenate([att_all[g] for g in range(grp)], axis=0)
    projected = lax.dot_general(
        lhs, w_v[...], (((1,), (1,)), ((), ())), preferred_element_type=jnp.float32
    )
    width = per * LANES
    for g in range(grp):
        for k in range(share):
            lo, hi = k * width, min((k + 1) * width, cols)
            if lo < hi:
                ps[g, k, :, 0 : hi - lo] = projected[g * slots : (g + 1) * slots, lo:hi].astype(
                    jnp.bfloat16
                )

    p_sends = []
    for a in range(grp):
        dst_g = lax.rem(j + a, grp)
        for k in range(share):
            dst_t = share * j + k
            copy = pltpu.make_async_remote_copy(
                src_ref=ps.at[dst_g, k],
                dst_ref=rs.at[t],
                send_sem=p_ssem.at[a, k],
                recv_sem=p_rsem.at[t],
                device_id=(dst_g, dst_t),
                device_id_type=MESH,
            )
            if a == 0:
                here = dst_t == t

                @pl.when(jnp.logical_not(here))
                def _():
                    copy.start()

                @pl.when(here)
                def _():
                    rs[t] = ps[j, k]

                p_sends.append((copy, here))
            else:
                copy.start()
                p_sends.append((copy, None))
    for d in range(tp):
        src = tp_src(d)
        copy = pltpu.make_async_remote_copy(
            src_ref=ps.at[0, 0],
            dst_ref=rs.at[src],
            send_sem=p_ssem.at[0, 0],
            recv_sem=p_rsem.at[src],
            device_id=(owner_grp, src),
            device_id_type=MESH,
        )
        if d == 0:

            @pl.when(jnp.logical_not(self_part))
            def _():
                copy.wait_recv()

        else:
            copy.wait_recv()
    total = rs[0].astype(jnp.float32)
    for src in range(1, tp):
        total = total + rs[src].astype(jnp.float32)
    red[...] = total.astype(jnp.bfloat16)

    o_sends = []
    for d in range(1, tp):
        copy = pltpu.make_async_remote_copy(
            src_ref=red,
            dst_ref=og.at[t],
            send_sem=o_ssem.at[d],
            recv_sem=o_rsem.at[t],
            device_id=(j, tp_peer(d)),
            device_id_type=MESH,
        )
        copy.start()
        o_sends.append(copy)
    og[t] = red[...]
    for copy in q_sends + part_sends + a_sends:
        copy.wait_send()
    for copy, here in p_sends:
        if here is None:
            copy.wait_send()
        else:

            @pl.when(jnp.logical_not(here))
            def _():
                copy.wait_send()

    for d in range(1, tp):
        src = tp_src(d)
        pltpu.make_async_remote_copy(
            src_ref=red,
            dst_ref=og.at[src],
            send_sem=o_ssem.at[d],
            recv_sem=o_rsem.at[src],
            device_id=(j, src),
            device_id_type=MESH,
        ).wait_recv()
    pieces = []
    for g in range(grp):
        for k in range(share):
            size = min((k + 1) * width, cols) - k * width
            if size > 0:
                pieces.append(og[g * share + k][:, :size].astype(jnp.float32))
    out_ref[0] = jnp.concatenate(pieces, axis=1)
    for copy in o_sends:
        copy.wait_send()


def local(tp, grp, batch_sizes, seq_lens, page_table, queries, kv_pool, new_kv, out_weight):
    out_weight = out_weight.T
    slots, pages = page_table.shape[1:]
    pool_pages, page_len, row_width = kv_pool.shape[1:]
    kv_heads = row_width // (2 * HD)
    own_width = queries.shape[2]
    own = own_width // HD
    heads = own * tp
    cols, rows = out_weight.shape
    share = tp // grp
    tiles = -(-cols // LANES)
    per = -(-tiles // share)
    half = slots // 2
    cfg = (tp, grp, heads, kv_heads, slots, pages, page_len, cols, per, share)
    bf16, f32 = jnp.bfloat16, jnp.float32
    sem = pltpu.SemaphoreType.DMA
    vmem, smem, hbm = (
        pl.BlockSpec(memory_space=pltpu.VMEM),
        pl.BlockSpec(memory_space=pltpu.SMEM),
        pl.BlockSpec(memory_space=pl.ANY),
    )
    return pl.pallas_call(
        functools.partial(fused_kernel, cfg),
        out_shape=jax.ShapeDtypeStruct((1, slots, cols * grp), f32),
        in_specs=[smem] + [hbm] * 6,
        out_specs=vmem,
        scratch_shapes=[
            pltpu.SMEM(seq_lens.shape, jnp.int32),
            pltpu.SMEM(page_table.shape, jnp.int32),
            pltpu.VMEM(new_kv.shape, bf16),
            pltpu.VMEM((pool_pages, page_len, row_width), bf16),
            pltpu.VMEM((cols, rows), bf16),
            pltpu.VMEM((tp, slots, own_width), bf16),
            pltpu.VMEM((kv_heads * HD // (2 * LANES), slots * heads, LANES), f32),
            pltpu.VMEM((heads * half, LANES), f32),
            pltpu.VMEM((tp, own * half, LANES), bf16),
            pltpu.VMEM((tp, own, LANES), f32),
            pltpu.VMEM((tp, own * half, LANES), bf16),
            pltpu.VMEM((tp, own, LANES), f32),
            pltpu.VMEM((grp, slots, own_width), bf16),
            pltpu.VMEM((grp, share, slots, per * LANES), bf16),
            pltpu.VMEM((tp, slots, per * LANES), bf16),
            pltpu.VMEM((slots, per * LANES), bf16),
            pltpu.VMEM((tp, slots, per * LANES), bf16),
            sem((POOL_CHUNKS + 5,)),
            sem((tp,)),
            sem((tp,)),
            sem((tp,)),
            sem((tp,)),
            sem((tp,)),
            sem((tp,)),
            sem((grp,)),
            sem((grp,)),
            sem((grp, share)),
            sem((tp,)),
            sem((tp,)),
            sem((tp,)),
        ],
        compiler_params=pltpu.CompilerParams(
            collective_id=0, has_side_effects=True, vmem_limit_bytes=60 * 1024 * 1024
        ),
        name="fused_decode",
    )(batch_sizes, seq_lens, page_table, queries, kv_pool, new_kv, out_weight)


def solution(mesh):
    return jax.shard_map(
        functools.partial(local, mesh.shape["tp"], mesh.shape["grp"]),
        mesh=mesh,
        in_specs=(
            P("grp"),
            P("grp", None),
            P("grp", None, "tp"),
            P("grp", None, "tp"),
            P("grp", "tp", None, None),
            P("grp", None, None),
            P("tp", "grp"),
        ),
        out_specs=P("grp", None, None),
        check_vma=False,
    )
```

```python
import functools

import jax
import jax.numpy as jnp
from jax import lax
from jax.experimental import pallas as pl
from jax.experimental.pallas import tpu as pltpu
from jax.sharding import PartitionSpec as P

HD = 64
LANES = 128
NEG_BIG = -1e30
POOL_CHUNKS = 8
MESH = pl.DeviceIdType.MESH


def fused_kernel(
    cfg,
    bs_ref,
    len_hbm,
    pt_hbm,
    q_hbm,
    kv_hbm,
    nkv_hbm,
    w_hbm,
    out_ref,
    len_ref,
    pt_ref,
    nkv_ref,
    kv_v,
    w_v,
    q_all,
    q_bd,
    wbuf,
    w_send,
    st_send,
    w_recv,
    st_recv,
    att_all,
    ps,
    rs,
    red,
    og,
    local_sem,
    q_ssem,
    q_rsem,
    w_ssem,
    w_rsem,
    st_ssem,
    st_rsem,
    a_ssem,
    a_rsem,
    p_ssem,
    p_rsem,
    o_ssem,
    o_rsem,
):
    tp, grp, heads, kv_heads, slots, pages, page_len, cols, per, share = cfg
    t = lax.axis_index("tp")
    j = lax.axis_index("grp")
    group_size = heads // kv_heads
    own = heads // tp
    half_slots = slots // 2
    half_kv = kv_heads // 2
    tokens = pages * page_len
    key_width = kv_heads * HD
    win = key_width // 2
    owner_grp = lax.div(t, share)
    self_part = owner_grp == j

    def tp_peer(d):
        return lax.rem(t + d, tp)

    def tp_src(d):
        return lax.rem(t + (tp - d), tp)

    quarter = group_size // 2

    def head_row(head):
        kv, g = head // group_size, head % group_size
        return (kv // 2) * 2 * group_size + (g % 2) * group_size + (kv % 2) * quarter + g // 2

    pool_pages = kv_v.shape[0]
    step = pool_pages // POOL_CHUNKS
    local = [
        pltpu.make_async_copy(
            kv_hbm.at[0, pl.ds(i * step, step)],
            kv_v.at[pl.ds(i * step, step)],
            local_sem.at[i],
        )
        for i in range(POOL_CHUNKS)
    ]
    w_copy = pltpu.make_async_copy(w_hbm, w_v, local_sem.at[POOL_CHUNKS])
    q_copy = pltpu.make_async_copy(q_hbm.at[0], q_all.at[t], local_sem.at[POOL_CHUNKS + 1])
    nkv_copy = pltpu.make_async_copy(nkv_hbm, nkv_ref, local_sem.at[POOL_CHUNKS + 2])
    len_copy = pltpu.make_async_copy(len_hbm, len_ref, local_sem.at[POOL_CHUNKS + 3])
    pt_copy = pltpu.make_async_copy(pt_hbm, pt_ref, local_sem.at[POOL_CHUNKS + 4])
    q_copy.start()
    nkv_copy.start()
    len_copy.start()
    pt_copy.start()
    for copy in local:
        copy.start()
    w_copy.start()

    barrier = pltpu.get_barrier_semaphore()
    for d in range(1, tp):
        pl.semaphore_signal(barrier, inc=1, device_id=(j, tp_peer(d)), device_id_type=MESH)
    for a in range(1, grp):
        pl.semaphore_signal(
            barrier, inc=1, device_id=(lax.rem(j + a, grp), t), device_id_type=MESH
        )
    q_bd[...] = jnp.zeros_like(q_bd)
    ps[...] = jnp.zeros_like(ps)
    pl.semaphore_wait(barrier, (tp - 1) + (grp - 1))

    q_sends = []
    for d in range(1, tp):
        copy = pltpu.make_async_remote_copy(
            src_ref=q_hbm.at[0],
            dst_ref=q_all.at[t],
            send_sem=q_ssem.at[d],
            recv_sem=q_rsem.at[t],
            device_id=(j, tp_peer(d)),
            device_id_type=MESH,
        )
        copy.start()
        q_sends.append(copy)
    q_copy.wait()
    nkv_copy.wait()

    lane = lax.broadcasted_iota(jnp.int32, (half_slots, LANES), 1)
    low = lane < HD

    kv_own = lax.div(t * own, group_size)
    odd = lax.rem(kv_own, 2)
    lane2 = lax.broadcasted_iota(jnp.int32, (slots, LANES), 1)
    low2 = lane2 < HD

    def kv_tile(base):
        start = pl.multiple_of(base + lax.div(kv_own, 2) * LANES, LANES)
        x = nkv_ref[0, :, pl.ds(start, LANES)].astype(jnp.float32)
        flipped = pltpu.roll(x, HD, 1)
        flip = jnp.broadcast_to(odd, x.shape) == 1
        first = jnp.where(flip, flipped, x)
        return jnp.where(low2, first, pltpu.roll(first, HD, 1))

    new_key = kv_tile(0)
    new_val = kv_tile(key_width)
    q_own = q_all[t].astype(jnp.float32)
    prod = q_own * jnp.concatenate([new_key] * (own // 2), axis=1)
    prod_hi = prod.astype(jnp.bfloat16)
    prod_lo = (prod - prod_hi.astype(jnp.float32)).astype(jnp.bfloat16)
    e_row = lax.broadcasted_iota(jnp.int32, (own * HD, LANES), 0) // HD
    e_col = lax.broadcasted_iota(jnp.int32, (own * HD, LANES), 1) % own
    e_row = (e_row % 2) * (own // 2) + e_row // 2
    spread = jnp.where(e_row == e_col, 1.0, 0.0).astype(jnp.bfloat16)
    self_score = jnp.dot(prod_hi, spread, preferred_element_type=jnp.float32) + jnp.dot(
        prod_lo, spread, preferred_element_type=jnp.float32
    )
    self_score = self_score * (HD**-0.5)

    for d in range(1, tp):
        src = tp_src(d)
        pltpu.make_async_remote_copy(
            src_ref=q_hbm.at[0],
            dst_ref=q_all.at[src],
            send_sem=q_ssem.at[d],
            recv_sem=q_rsem.at[src],
            device_id=(j, src),
            device_id_type=MESH,
        ).wait_recv()
    for src in range(tp):
        rows = q_all[src].astype(jnp.float32) * (HD**-0.5)
        for pair in range(own // 2):
            tile = rows[:, pair * LANES : (pair + 1) * LANES]
            turned = pltpu.roll(tile, HD, 1)
            for side in range(2):
                head = src * own + pair * 2 + side
                kv = head // group_size
                value = tile if side == kv % 2 else turned
                keep = low2 if kv % 2 == 0 else jnp.logical_not(low2)
                value = jnp.where(keep, value, 0.0)
                row = head_row(head)
                q_bd[(kv % half_kv) // 2, pl.ds(row, slots, stride=heads), :] = value

    len_copy.wait()
    pt_copy.wait()
    for copy in local:
        copy.wait()

    col = lax.broadcasted_iota(jnp.int32, (heads, tokens), 1)
    position = ((col // page_len) * tp + t) * page_len + col % page_len
    stat_lane = lax.broadcasted_iota(jnp.int32, (heads, LANES), 1)
    tiles_in_win = win // LANES
    rows_in_win = half_kv * group_size

    def one_slot(s):
        first = pl.multiple_of(s * heads, heads)
        ids = [pt_ref[0, s, i] for i in range(pages)]
        length = len_ref[0, s]

        def block(start):
            return jnp.concatenate(
                [kv_v[ids[i], :, start : start + win] for i in range(pages)], axis=0
            )

        scores = []
        for w in range(2):
            q_w = jnp.concatenate(
                [
                    q_bd[k, pl.ds(first + w * rows_in_win, rows_in_win), :]
                    for k in range(tiles_in_win)
                ],
                axis=1,
            ).astype(jnp.bfloat16)
            scores.append(
                lax.dot_general(
                    q_w,
                    block(w * win),
                    (((1,), (1,)), ((), ())),
                    preferred_element_type=jnp.float32,
                )
            )
        scores = jnp.concatenate(scores, axis=0)
        valid = position < length
        scores = jnp.where(valid, scores, NEG_BIG)
        top = jnp.max(scores, axis=1, keepdims=True)
        weights = jnp.where(valid, jnp.exp(scores - top), 0.0)
        total = jnp.sum(weights, axis=1, keepdims=True)
        rounded = weights.astype(jnp.bfloat16)
        tiles = []
        for w in range(2):
            o = jnp.dot(
                rounded[w * rows_in_win : (w + 1) * rows_in_win],
                block(key_width + w * win),
                preferred_element_type=jnp.float32,
            )
            for k in range(tiles_in_win):
                base = k * 2 * group_size
                lanes = slice(k * LANES, (k + 1) * LANES)
                a = o[base : base + group_size, lanes]
                b = o[base + group_size : base + 2 * group_size, lanes]
                a = jnp.where(upper, a, pltpu.roll(a, HD, 1))
                b = jnp.where(upper, pltpu.roll(b, HD, 1), b)
                tiles.append(jnp.where(g_low, a, b))
        return tiles, top, total

    g_low = lax.broadcasted_iota(jnp.int32, (group_size, LANES), 1) < HD
    upper = lax.broadcasted_iota(jnp.int32, (group_size, LANES), 0) < quarter
    hs = half_slots
    pairs = own // 2
    span = pairs * hs

    def attend_half(h):
        def body(i, stats):
            for off in (0, hs // 2):
                r = i + off
                tiles, top, total = one_slot(h * hs + r)
                for k in range(kv_heads // 2):
                    wbuf[pl.ds(k * group_size * hs + r, group_size, stride=hs), :] = tiles[k]
                stats = jnp.where(stat_lane == r, top, stats)
                stats = jnp.where(stat_lane == r + hs, total, stats)
            return stats

        stats = lax.fori_loop(0, hs // 2, body, jnp.zeros((heads, LANES), jnp.float32))
        for dst in range(tp):
            w_send[h, dst] = wbuf[dst * span : (dst + 1) * span, :].astype(jnp.bfloat16)
            for p in range(2):
                row = head_row(dst * own + p)
                st_send[h, dst, p * pairs : (p + 1) * pairs] = stats[row : row + pairs]

    def exchange(src_of, dst_buf, ssem, rsem, h):
        sends = []
        for d in range(1, tp):
            peer = tp_peer(d)
            copy = pltpu.make_async_remote_copy(
                src_ref=src_of(peer),
                dst_ref=dst_buf.at[h, t],
                send_sem=ssem.at[h, d],
                recv_sem=rsem.at[h, t],
                device_id=(j, peer),
                device_id_type=MESH,
            )
            copy.start()
            sends.append(copy)
        return sends

    def arrive(src_of, dst_buf, ssem, rsem, h):
        for d in range(1, tp):
            src = tp_src(d)
            pltpu.make_async_remote_copy(
                src_ref=src_of(src),
                dst_ref=dst_buf.at[h, src],
                send_sem=ssem.at[h, d],
                recv_sem=rsem.at[h, src],
                device_id=(j, src),
                device_id_type=MESH,
            ).wait_recv()

    def across(x, op):
        shift = own
        while shift < heads:
            x = op(x, pltpu.roll(x, shift, 1))
            shift *= 2
        return x

    def pair_cast(x, base, q):
        a, b = base + q, base + pairs + q
        return jnp.where(
            low,
            jnp.broadcast_to(x[:, a : a + 1], (hs, LANES)),
            jnp.broadcast_to(x[:, b : b + 1], (hs, LANES)),
        )

    def combine_half(h):
        arrive(lambda p: st_send.at[h, p], st_recv, st_ssem, st_rsem, h)
        stacked = jnp.concatenate(
            [st_recv[h, src] for src in range(tp)] * (LANES // heads), axis=0
        )
        turned = jnp.transpose(stacked)
        top, total = turned[:hs], turned[hs : 2 * hs]
        self_h = self_score[h * hs : (h + 1) * hs]
        final = jnp.maximum(across(top, jnp.maximum), self_h)
        scale = jnp.exp(top - final)
        self_w = jnp.exp(self_h - final)
        denominator = across(scale * total, jnp.add) + self_w
        part = scale / denominator
        own_part = self_w / denominator
        value = new_val[h * hs : (h + 1) * hs]
        sums = [pair_cast(own_part, 0, q) * value for q in range(pairs)]
        factors = [[pair_cast(part, src * own, q) for q in range(pairs)] for src in range(tp)]
        arrive(lambda p: w_send.at[h, p], w_recv, w_ssem, w_rsem, h)
        for src in range(tp):
            block = w_recv[h, src].astype(jnp.float32)
            for q in range(pairs):
                sums[q] = sums[q] + factors[src][q] * block[q * hs : (q + 1) * hs]
        attended = jnp.concatenate(sums, axis=1)
        slot_row = lax.broadcasted_iota(jnp.int32, attended.shape, 0) + h * hs
        attended = jnp.where(slot_row < bs_ref[0], attended, 0.0).astype(jnp.bfloat16)
        att_all[h, j] = attended
        sends = []
        for a in range(1, grp):
            copy = pltpu.make_async_remote_copy(
                src_ref=att_all.at[h, j],
                dst_ref=att_all.at[h, j],
                send_sem=a_ssem.at[h, a],
                recv_sem=a_rsem.at[h, j],
                device_id=(lax.rem(j + a, grp), t),
                device_id_type=MESH,
            )
            copy.start()
            sends.append(copy)
        return sends

    width = per * LANES

    def project_half(h):
        for a in range(1, grp):
            src = lax.rem(j + (grp - a), grp)
            pltpu.make_async_remote_copy(
                src_ref=att_all.at[h, src],
                dst_ref=att_all.at[h, src],
                send_sem=a_ssem.at[h, a],
                recv_sem=a_rsem.at[h, src],
                device_id=(src, t),
                device_id_type=MESH,
            ).wait_recv()
        lhs = jnp.concatenate([att_all[h, g] for g in range(grp)], axis=0)
        projected = lax.dot_general(
            lhs, w_v[...], (((1,), (1,)), ((), ())), preferred_element_type=jnp.float32
        )
        for g in range(grp):
            for k in range(share):
                lo, hi = k * width, min((k + 1) * width, cols)
                if lo < hi:
                    ps[h, g, k, :, 0 : hi - lo] = projected[
                        g * hs : (g + 1) * hs, lo:hi
                    ].astype(jnp.bfloat16)
        sends = []
        for a in range(grp):
            dst_g = lax.rem(j + a, grp)
            for k in range(share):
                dst_t = share * j + k
                copy = pltpu.make_async_remote_copy(
                    src_ref=ps.at[h, dst_g, k],
                    dst_ref=rs.at[h, t],
                    send_sem=p_ssem.at[h, a, k],
                    recv_sem=p_rsem.at[h, t],
                    device_id=(dst_g, dst_t),
                    device_id_type=MESH,
                )
                if a == 0:
                    here = dst_t == t

                    @pl.when(jnp.logical_not(here))
                    def _():
                        copy.start()

                    @pl.when(here)
                    def _():
                        rs[h, t] = ps[h, j, k]

                    sends.append((copy, here))
                else:
                    copy.start()
                    sends.append((copy, None))
        return sends

    def sum_half(h):
        for d in range(tp):
            src = tp_src(d)
            copy = pltpu.make_async_remote_copy(
                src_ref=ps.at[h, 0, 0],
                dst_ref=rs.at[h, src],
                send_sem=p_ssem.at[h, 0, 0],
                recv_sem=p_rsem.at[h, src],
                device_id=(owner_grp, src),
                device_id_type=MESH,
            )
            if d == 0:

                @pl.when(jnp.logical_not(self_part))
                def _():
                    copy.wait_recv()

            else:
                copy.wait_recv()
        total = rs[h, 0].astype(jnp.float32)
        for src in range(1, tp):
            total = total + rs[h, src].astype(jnp.float32)
        red[h] = total.astype(jnp.bfloat16)
        sends = exchange(lambda p: red.at[h], og, o_ssem, o_rsem, h)
        og[h, t] = red[h]
        return sends

    sends, p_sends = list(q_sends), []
    for h in range(2):
        attend_half(h)
        sends += exchange(lambda p: st_send.at[h, p], st_recv, st_ssem, st_rsem, h)
        sends += exchange(lambda p: w_send.at[h, p], w_recv, w_ssem, w_rsem, h)
        w_recv[h, t] = w_send[h, t]
        st_recv[h, t] = st_send[h, t]
    w_copy.wait()
    for h in range(2):
        sends += combine_half(h)
    for h in range(2):
        p_sends += project_half(h)
    for h in range(2):
        sends += sum_half(h)
    for h in range(2):
        arrive(lambda p: red.at[h], og, o_ssem, o_rsem, h)
        pieces = []
        for g in range(grp):
            for k in range(share):
                size = min((k + 1) * width, cols) - k * width
                if size > 0:
                    pieces.append(og[h, g * share + k][:, :size].astype(jnp.float32))
        out_ref[0, h * hs : (h + 1) * hs] = jnp.concatenate(pieces, axis=1)
    for copy in sends:
        copy.wait_send()
    for copy, here in p_sends:
        if here is None:
            copy.wait_send()
        else:

            @pl.when(jnp.logical_not(here))
            def _():
                copy.wait_send()


def local(tp, grp, batch_sizes, seq_lens, page_table, queries, kv_pool, new_kv, out_weight):
    out_weight = out_weight.T
    slots, pages = page_table.shape[1:]
    pool_pages, page_len, row_width = kv_pool.shape[1:]
    kv_heads = row_width // (2 * HD)
    own_width = queries.shape[2]
    own = own_width // HD
    heads = own * tp
    cols, rows = out_weight.shape
    share = tp // grp
    tiles = -(-cols // LANES)
    per = -(-tiles // share)
    half = slots // 2
    cfg = (tp, grp, heads, kv_heads, slots, pages, page_len, cols, per, share)
    bf16, f32 = jnp.bfloat16, jnp.float32
    sem = pltpu.SemaphoreType.DMA
    vmem, smem, hbm = (
        pl.BlockSpec(memory_space=pltpu.VMEM),
        pl.BlockSpec(memory_space=pltpu.SMEM),
        pl.BlockSpec(memory_space=pl.ANY),
    )
    return pl.pallas_call(
        functools.partial(fused_kernel, cfg),
        out_shape=jax.ShapeDtypeStruct((1, slots, cols * grp), f32),
        in_specs=[smem] + [hbm] * 6,
        out_specs=vmem,
        scratch_shapes=[
            pltpu.SMEM(seq_lens.shape, jnp.int32),
            pltpu.SMEM(page_table.shape, jnp.int32),
            pltpu.VMEM(new_kv.shape, bf16),
            pltpu.VMEM((pool_pages, page_len, row_width), bf16),
            pltpu.VMEM((cols, rows), bf16),
            pltpu.VMEM((tp, slots, own_width), bf16),
            pltpu.VMEM((kv_heads * HD // (2 * LANES), slots * heads, LANES), f32),
            pltpu.VMEM((heads * half // 2, LANES), f32),
            pltpu.VMEM((2, tp, own // 2 * half, LANES), bf16),
            pltpu.VMEM((2, tp, own, LANES), f32),
            pltpu.VMEM((2, tp, own // 2 * half, LANES), bf16),
            pltpu.VMEM((2, tp, own, LANES), f32),
            pltpu.VMEM((2, grp, half, own_width), bf16),
            pltpu.VMEM((2, grp, share, half, per * LANES), bf16),
            pltpu.VMEM((2, tp, half, per * LANES), bf16),
            pltpu.VMEM((2, half, per * LANES), bf16),
            pltpu.VMEM((2, tp, half, per * LANES), bf16),
            sem((POOL_CHUNKS + 5,)),
            sem((tp,)),
            sem((tp,)),
            sem((2, tp)),
            sem((2, tp)),
            sem((2, tp)),
            sem((2, tp)),
            sem((2, grp)),
            sem((2, grp)),
            sem((2, grp, share)),
            sem((2, tp)),
            sem((2, tp)),
            sem((2, tp)),
        ],
        compiler_params=pltpu.CompilerParams(
            collective_id=0, has_side_effects=True, vmem_limit_bytes=60 * 1024 * 1024
        ),
        name="fused_decode",
    )(batch_sizes, seq_lens, page_table, queries, kv_pool, new_kv, out_weight)


def solution(mesh):
    return jax.shard_map(
        functools.partial(local, mesh.shape["tp"], mesh.shape["grp"]),
        mesh=mesh,
        in_specs=(
            P("grp"),
            P("grp", None),
            P("grp", None, "tp"),
            P("grp", None, "tp"),
            P("grp", "tp", None, None),
            P("grp", None, None),
            P("tp", "grp"),
        ),
        out_specs=P("grp", None, None),
        check_vma=False,
    )
```

```python
import functools

import jax
import jax.numpy as jnp
from jax import lax
from jax.experimental import pallas as pl
from jax.experimental.pallas import tpu as pltpu
from jax.sharding import PartitionSpec as P

HD = 64
LANES = 128
NEG_BIG = -1e30
POOL_CHUNKS = 8
MESH = pl.DeviceIdType.MESH


def fused_kernel(
    cfg,
    bs_ref,
    len_hbm,
    pt_hbm,
    q_hbm,
    kv_hbm,
    nkv_hbm,
    w_hbm,
    out_ref,
    len_ref,
    pt_ref,
    nkv_ref,
    kv_v,
    w_v,
    q_all,
    q_bd,
    wbuf,
    w_send,
    st_send,
    w_recv,
    st_recv,
    att_all,
    ps,
    rs,
    red,
    og,
    local_sem,
    q_ssem,
    q_rsem,
    w_ssem,
    w_rsem,
    st_ssem,
    st_rsem,
    a_ssem,
    a_rsem,
    p_ssem,
    p_rsem,
    o_ssem,
    o_rsem,
):
    tp, grp, heads, kv_heads, slots, pages, page_len, cols, per, share = cfg
    t = lax.axis_index("tp")
    j = lax.axis_index("grp")
    group_size = heads // kv_heads
    own = heads // tp
    half_slots = slots // 2
    half_kv = kv_heads // 2
    tokens = pages * page_len
    key_width = kv_heads * HD
    win = key_width // 2
    owner_grp = lax.div(t, share)
    self_part = owner_grp == j

    def tp_peer(d):
        return lax.rem(t + d, tp)

    def tp_src(d):
        return lax.rem(t + (tp - d), tp)

    quarter = group_size // 2

    def head_row(head):
        kv, g = head // group_size, head % group_size
        return (kv // 2) * 2 * group_size + (g % 2) * group_size + (kv % 2) * quarter + g // 2

    barrier = pltpu.get_barrier_semaphore()
    for d in range(1, tp):
        pl.semaphore_signal(barrier, inc=1, device_id=(j, tp_peer(d)), device_id_type=MESH)
    for a in range(1, grp):
        pl.semaphore_signal(
            barrier, inc=1, device_id=(lax.rem(j + a, grp), t), device_id_type=MESH
        )

    pool_pages = kv_v.shape[0]
    step = pool_pages // POOL_CHUNKS
    local = [
        pltpu.make_async_copy(
            kv_hbm.at[0, pl.ds(i * step, step)],
            kv_v.at[pl.ds(i * step, step)],
            local_sem.at[i],
        )
        for i in range(POOL_CHUNKS)
    ]
    w_copy = pltpu.make_async_copy(w_hbm, w_v, local_sem.at[POOL_CHUNKS])
    q_copy = pltpu.make_async_copy(q_hbm.at[0], q_all.at[t], local_sem.at[POOL_CHUNKS + 1])
    nkv_copy = pltpu.make_async_copy(nkv_hbm, nkv_ref, local_sem.at[POOL_CHUNKS + 2])
    len_copy = pltpu.make_async_copy(len_hbm, len_ref, local_sem.at[POOL_CHUNKS + 3])
    pt_copy = pltpu.make_async_copy(pt_hbm, pt_ref, local_sem.at[POOL_CHUNKS + 4])
    q_copy.start()
    nkv_copy.start()
    len_copy.start()
    pt_copy.start()
    for copy in local:
        copy.start()
    w_copy.start()

    q_bd[...] = jnp.zeros_like(q_bd)
    ps[...] = jnp.zeros_like(ps)
    pl.semaphore_wait(barrier, (tp - 1) + (grp - 1))

    q_sends = []
    for d in range(1, tp):
        copy = pltpu.make_async_remote_copy(
            src_ref=q_hbm.at[0],
            dst_ref=q_all.at[t],
            send_sem=q_ssem.at[d],
            recv_sem=q_rsem.at[t],
            device_id=(j, tp_peer(d)),
            device_id_type=MESH,
        )
        copy.start()
        q_sends.append(copy)
    q_copy.wait()
    nkv_copy.wait()

    lane = lax.broadcasted_iota(jnp.int32, (half_slots, LANES), 1)
    low = lane < HD

    kv_own = lax.div(t * own, group_size)
    odd = lax.rem(kv_own, 2)
    lane2 = lax.broadcasted_iota(jnp.int32, (slots, LANES), 1)
    low2 = lane2 < HD

    def kv_tile(base):
        start = pl.multiple_of(base + lax.div(kv_own, 2) * LANES, LANES)
        x = nkv_ref[0, :, pl.ds(start, LANES)].astype(jnp.float32)
        flipped = pltpu.roll(x, HD, 1)
        flip = jnp.broadcast_to(odd, x.shape) == 1
        first = jnp.where(flip, flipped, x)
        return jnp.where(low2, first, pltpu.roll(first, HD, 1))

    new_key = kv_tile(0)
    new_val = kv_tile(key_width)
    q_own = q_all[t].astype(jnp.float32)
    prod = q_own * jnp.concatenate([new_key] * (own // 2), axis=1)
    prod_hi = prod.astype(jnp.bfloat16)
    prod_lo = (prod - prod_hi.astype(jnp.float32)).astype(jnp.bfloat16)
    e_row = lax.broadcasted_iota(jnp.int32, (own * HD, LANES), 0) // HD
    e_col = lax.broadcasted_iota(jnp.int32, (own * HD, LANES), 1) % own
    e_row = (e_row % 2) * (own // 2) + e_row // 2
    spread = jnp.where(e_row == e_col, 1.0, 0.0).astype(jnp.bfloat16)
    self_score = jnp.dot(prod_hi, spread, preferred_element_type=jnp.float32) + jnp.dot(
        prod_lo, spread, preferred_element_type=jnp.float32
    )
    self_score = self_score * (HD**-0.5)

    for d in range(1, tp):
        src = tp_src(d)
        pltpu.make_async_remote_copy(
            src_ref=q_hbm.at[0],
            dst_ref=q_all.at[src],
            send_sem=q_ssem.at[d],
            recv_sem=q_rsem.at[src],
            device_id=(j, src),
            device_id_type=MESH,
        ).wait_recv()
    for src in range(tp):
        rows = q_all[src].astype(jnp.float32) * (HD**-0.5)
        for pair in range(own // 2):
            tile = rows[:, pair * LANES : (pair + 1) * LANES]
            turned = pltpu.roll(tile, HD, 1)
            for side in range(2):
                head = src * own + pair * 2 + side
                kv = head // group_size
                value = tile if side == kv % 2 else turned
                keep = low2 if kv % 2 == 0 else jnp.logical_not(low2)
                value = jnp.where(keep, value, 0.0)
                row = head_row(head)
                q_bd[(kv % half_kv) // 2, pl.ds(row, slots, stride=heads), :] = value

    len_copy.wait()
    pt_copy.wait()
    for copy in local:
        copy.wait()

    col = lax.broadcasted_iota(jnp.int32, (heads, tokens), 1)
    position = ((col // page_len) * tp + t) * page_len + col % page_len
    stat_lane = lax.broadcasted_iota(jnp.int32, (heads, LANES), 1)
    tiles_in_win = win // LANES
    rows_in_win = half_kv * group_size

    def slot_scores(s):
        first = s * heads
        ids = [pt_ref[0, s, i] for i in range(pages)]
        length = len_ref[0, s]

        def block(start):
            return jnp.concatenate(
                [kv_v[ids[i], :, start : start + win] for i in range(pages)], axis=0
            )

        scores = []
        for w in range(2):
            q_w = jnp.concatenate(
                [
                    q_bd[k, pl.ds(first + w * rows_in_win, rows_in_win), :]
                    for k in range(tiles_in_win)
                ],
                axis=1,
            ).astype(jnp.bfloat16)
            scores.append(
                lax.dot_general(
                    q_w,
                    block(w * win),
                    (((1,), (1,)), ((), ())),
                    preferred_element_type=jnp.float32,
                )
            )
        return jnp.concatenate(scores, axis=0), block, length

    def slot_values(scores, block, length):
        valid = position < length
        scores = jnp.where(valid, scores, NEG_BIG)
        top = jnp.max(scores, axis=1, keepdims=True)
        weights = jnp.where(valid, jnp.exp(scores - top), 0.0)
        total = jnp.sum(weights, axis=1, keepdims=True)
        rounded = weights.astype(jnp.bfloat16)
        tiles = []
        for w in range(2):
            o = jnp.dot(
                rounded[w * rows_in_win : (w + 1) * rows_in_win],
                block(key_width + w * win),
                preferred_element_type=jnp.float32,
            )
            for k in range(tiles_in_win):
                base = k * 2 * group_size
                lanes = slice(k * LANES, (k + 1) * LANES)
                a = o[base : base + group_size, lanes]
                b = o[base + group_size : base + 2 * group_size, lanes]
                a = jnp.where(upper, a, pltpu.roll(a, HD, 1))
                b = jnp.where(upper, pltpu.roll(b, HD, 1), b)
                tiles.append(jnp.where(g_low, a, b))
        return tiles, top, total

    g_low = lax.broadcasted_iota(jnp.int32, (group_size, LANES), 1) < HD
    upper = lax.broadcasted_iota(jnp.int32, (group_size, LANES), 0) < quarter
    hs = half_slots
    pairs = own // 2
    span = pairs * hs

    def attend_half(h):
        stats = jnp.zeros((heads, LANES), jnp.float32)
        staged = [slot_scores(h * hs)]
        for r in range(hs):
            if r + 1 < hs:
                staged.append(slot_scores(h * hs + r + 1))
            tiles, top, total = slot_values(*staged[r])
            for k in range(kv_heads // 2):
                wbuf[pl.ds(k * group_size * hs + r, group_size, stride=hs), :] = tiles[k]
            stats = jnp.where(stat_lane == r, top, stats)
            stats = jnp.where(stat_lane == r + hs, total, stats)
        for dst in range(tp):
            w_send[h, dst] = wbuf[dst * span : (dst + 1) * span, :].astype(jnp.bfloat16)
            for p in range(2):
                row = head_row(dst * own + p)
                st_send[h, dst, p * pairs : (p + 1) * pairs] = stats[row : row + pairs]

    def exchange(src_of, dst_buf, ssem, rsem, h):
        sends = []
        for d in range(1, tp):
            peer = tp_peer(d)
            copy = pltpu.make_async_remote_copy(
                src_ref=src_of(peer),
                dst_ref=dst_buf.at[h, t],
                send_sem=ssem.at[h, d],
                recv_sem=rsem.at[h, t],
                device_id=(j, peer),
                device_id_type=MESH,
            )
            copy.start()
            sends.append(copy)
        return sends

    def arrive(src_of, dst_buf, ssem, rsem, h):
        for d in range(1, tp):
            src = tp_src(d)
            pltpu.make_async_remote_copy(
                src_ref=src_of(src),
                dst_ref=dst_buf.at[h, src],
                send_sem=ssem.at[h, d],
                recv_sem=rsem.at[h, src],
                device_id=(j, src),
                device_id_type=MESH,
            ).wait_recv()

    def across(x, op):
        shift = own
        while shift < heads:
            x = op(x, pltpu.roll(x, shift, 1))
            shift *= 2
        return x

    def pair_cast(x, base, q):
        a, b = base + q, base + pairs + q
        return jnp.where(
            low,
            jnp.broadcast_to(x[:, a : a + 1], (hs, LANES)),
            jnp.broadcast_to(x[:, b : b + 1], (hs, LANES)),
        )

    def combine_half(h):
        arrive(lambda p: st_send.at[h, p], st_recv, st_ssem, st_rsem, h)
        stacked = jnp.concatenate(
            [st_recv[h, src] for src in range(tp)] * (LANES // heads), axis=0
        )
        turned = jnp.transpose(stacked)
        top, total = turned[:hs], turned[hs : 2 * hs]
        self_h = self_score[h * hs : (h + 1) * hs]
        final = jnp.maximum(across(top, jnp.maximum), self_h)
        scale = jnp.exp(top - final)
        self_w = jnp.exp(self_h - final)
        denominator = across(scale * total, jnp.add) + self_w
        part = scale / denominator
        own_part = self_w / denominator
        value = new_val[h * hs : (h + 1) * hs]
        sums = [pair_cast(own_part, 0, q) * value for q in range(pairs)]
        factors = [[pair_cast(part, src * own, q) for q in range(pairs)] for src in range(tp)]
        arrive(lambda p: w_send.at[h, p], w_recv, w_ssem, w_rsem, h)
        for src in range(tp):
            block = w_recv[h, src].astype(jnp.float32)
            for q in range(pairs):
                sums[q] = sums[q] + factors[src][q] * block[q * hs : (q + 1) * hs]
        attended = jnp.concatenate(sums, axis=1)
        slot_row = lax.broadcasted_iota(jnp.int32, attended.shape, 0) + h * hs
        attended = jnp.where(slot_row < bs_ref[0], attended, 0.0).astype(jnp.bfloat16)
        att_all[h, j] = attended
        sends = []
        for a in range(1, grp):
            copy = pltpu.make_async_remote_copy(
                src_ref=att_all.at[h, j],
                dst_ref=att_all.at[h, j],
                send_sem=a_ssem.at[h, a],
                recv_sem=a_rsem.at[h, j],
                device_id=(lax.rem(j + a, grp), t),
                device_id_type=MESH,
            )
            copy.start()
            sends.append(copy)
        return sends

    width = per * LANES

    def project_half(h):
        for a in range(1, grp):
            src = lax.rem(j + (grp - a), grp)
            pltpu.make_async_remote_copy(
                src_ref=att_all.at[h, src],
                dst_ref=att_all.at[h, src],
                send_sem=a_ssem.at[h, a],
                recv_sem=a_rsem.at[h, src],
                device_id=(src, t),
                device_id_type=MESH,
            ).wait_recv()
        lhs = jnp.concatenate([att_all[h, g] for g in range(grp)], axis=0)
        projected = lax.dot_general(
            lhs, w_v[...], (((1,), (1,)), ((), ())), preferred_element_type=jnp.float32
        )
        for g in range(grp):
            for k in range(share):
                lo, hi = k * width, min((k + 1) * width, cols)
                if lo < hi:
                    ps[h, g, k, :, 0 : hi - lo] = projected[
                        g * hs : (g + 1) * hs, lo:hi
                    ].astype(jnp.bfloat16)
        sends = []
        for a in range(grp):
            dst_g = lax.rem(j + a, grp)
            for k in range(share):
                dst_t = share * j + k
                copy = pltpu.make_async_remote_copy(
                    src_ref=ps.at[h, dst_g, k],
                    dst_ref=rs.at[h, t],
                    send_sem=p_ssem.at[h, a, k],
                    recv_sem=p_rsem.at[h, t],
                    device_id=(dst_g, dst_t),
                    device_id_type=MESH,
                )
                if a == 0:
                    here = dst_t == t

                    @pl.when(jnp.logical_not(here))
                    def _():
                        copy.start()

                    @pl.when(here)
                    def _():
                        rs[h, t] = ps[h, j, k]

                    sends.append((copy, here))
                else:
                    copy.start()
                    sends.append((copy, None))
        return sends

    def sum_half(h):
        for d in range(tp):
            src = tp_src(d)
            copy = pltpu.make_async_remote_copy(
                src_ref=ps.at[h, 0, 0],
                dst_ref=rs.at[h, src],
                send_sem=p_ssem.at[h, 0, 0],
                recv_sem=p_rsem.at[h, src],
                device_id=(owner_grp, src),
                device_id_type=MESH,
            )
            if d == 0:

                @pl.when(jnp.logical_not(self_part))
                def _():
                    copy.wait_recv()

            else:
                copy.wait_recv()
        total = rs[h, 0].astype(jnp.float32)
        for src in range(1, tp):
            total = total + rs[h, src].astype(jnp.float32)
        red[h] = total.astype(jnp.bfloat16)
        sends = exchange(lambda p: red.at[h], og, o_ssem, o_rsem, h)
        og[h, t] = red[h]
        return sends

    sends, p_sends = list(q_sends), []
    for h in range(2):
        attend_half(h)
        sends += exchange(lambda p: st_send.at[h, p], st_recv, st_ssem, st_rsem, h)
        sends += exchange(lambda p: w_send.at[h, p], w_recv, w_ssem, w_rsem, h)
        w_recv[h, t] = w_send[h, t]
        st_recv[h, t] = st_send[h, t]
    w_copy.wait()
    for h in range(2):
        sends += combine_half(h)
    for h in range(2):
        p_sends += project_half(h)
    for h in range(2):
        sends += sum_half(h)
    for h in range(2):
        arrive(lambda p: red.at[h], og, o_ssem, o_rsem, h)
        pieces = []
        for g in range(grp):
            for k in range(share):
                size = min((k + 1) * width, cols) - k * width
                if size > 0:
                    pieces.append(og[h, g * share + k][:, :size].astype(jnp.float32))
        out_ref[0, h * hs : (h + 1) * hs] = jnp.concatenate(pieces, axis=1)
    for copy in sends:
        copy.wait_send()
    for copy, here in p_sends:
        if here is None:
            copy.wait_send()
        else:

            @pl.when(jnp.logical_not(here))
            def _():
                copy.wait_send()


def local(tp, grp, batch_sizes, seq_lens, page_table, queries, kv_pool, new_kv, out_weight):
    out_weight = out_weight.T
    slots, pages = page_table.shape[1:]
    pool_pages, page_len, row_width = kv_pool.shape[1:]
    kv_heads = row_width // (2 * HD)
    own_width = queries.shape[2]
    own = own_width // HD
    heads = own * tp
    cols, rows = out_weight.shape
    share = tp // grp
    tiles = -(-cols // LANES)
    per = -(-tiles // share)
    half = slots // 2
    cfg = (tp, grp, heads, kv_heads, slots, pages, page_len, cols, per, share)
    bf16, f32 = jnp.bfloat16, jnp.float32
    sem = pltpu.SemaphoreType.DMA
    vmem, smem, hbm = (
        pl.BlockSpec(memory_space=pltpu.VMEM),
        pl.BlockSpec(memory_space=pltpu.SMEM),
        pl.BlockSpec(memory_space=pl.ANY),
    )
    return pl.pallas_call(
        functools.partial(fused_kernel, cfg),
        out_shape=jax.ShapeDtypeStruct((1, slots, cols * grp), f32),
        in_specs=[smem] + [hbm] * 6,
        out_specs=vmem,
        scratch_shapes=[
            pltpu.SMEM(seq_lens.shape, jnp.int32),
            pltpu.SMEM(page_table.shape, jnp.int32),
            pltpu.VMEM(new_kv.shape, bf16),
            pltpu.VMEM((pool_pages, page_len, row_width), bf16),
            pltpu.VMEM((cols, rows), bf16),
            pltpu.VMEM((tp, slots, own_width), bf16),
            pltpu.VMEM((kv_heads * HD // (2 * LANES), slots * heads, LANES), f32),
            pltpu.VMEM((heads * half // 2, LANES), f32),
            pltpu.VMEM((2, tp, own // 2 * half, LANES), bf16),
            pltpu.VMEM((2, tp, own, LANES), f32),
            pltpu.VMEM((2, tp, own // 2 * half, LANES), bf16),
            pltpu.VMEM((2, tp, own, LANES), f32),
            pltpu.VMEM((2, grp, half, own_width), bf16),
            pltpu.VMEM((2, grp, share, half, per * LANES), bf16),
            pltpu.VMEM((2, tp, half, per * LANES), bf16),
            pltpu.VMEM((2, half, per * LANES), bf16),
            pltpu.VMEM((2, tp, half, per * LANES), bf16),
            sem((POOL_CHUNKS + 5,)),
            sem((tp,)),
            sem((tp,)),
            sem((2, tp)),
            sem((2, tp)),
            sem((2, tp)),
            sem((2, tp)),
            sem((2, grp)),
            sem((2, grp)),
            sem((2, grp, share)),
            sem((2, tp)),
            sem((2, tp)),
            sem((2, tp)),
        ],
        compiler_params=pltpu.CompilerParams(
            collective_id=0, has_side_effects=True, vmem_limit_bytes=60 * 1024 * 1024
        ),
        name="fused_decode",
    )(batch_sizes, seq_lens, page_table, queries, kv_pool, new_kv, out_weight)


def solution(mesh):
    return jax.shard_map(
        functools.partial(local, mesh.shape["tp"], mesh.shape["grp"]),
        mesh=mesh,
        in_specs=(
            P("grp"),
            P("grp", None),
            P("grp", None, "tp"),
            P("grp", None, "tp"),
            P("grp", "tp", None, None),
            P("grp", None, None),
            P("tp", "grp"),
        ),
        out_specs=P("grp", None, None),
        check_vma=False,
    )
```

```python
import functools

import jax
import jax.numpy as jnp
from jax import lax
from jax.experimental import pallas as pl
from jax.experimental.pallas import tpu as pltpu
from jax.sharding import PartitionSpec as P

HD = 64
LANES = 128
NEG_BIG = -1e30
POOL_CHUNKS = 8
MESH = pl.DeviceIdType.MESH


def fused_kernel(
    cfg,
    bs_ref,
    len_hbm,
    pt_hbm,
    q_hbm,
    kv_hbm,
    nkv_hbm,
    w_hbm,
    out_ref,
    len_ref,
    pt_ref,
    nkv_ref,
    kv_v,
    w_v,
    q_all,
    q_bd,
    wbuf,
    w_send,
    st_send,
    w_recv,
    st_recv,
    att_all,
    ps,
    rs,
    red,
    og,
    local_sem,
    q_ssem,
    q_rsem,
    w_ssem,
    w_rsem,
    st_ssem,
    st_rsem,
    a_ssem,
    a_rsem,
    p_ssem,
    p_rsem,
    o_ssem,
    o_rsem,
):
    tp, grp, heads, kv_heads, slots, pages, page_len, cols, per, share = cfg
    t = lax.axis_index("tp")
    j = lax.axis_index("grp")
    group_size = heads // kv_heads
    own = heads // tp
    half_slots = slots // 2
    half_kv = kv_heads // 2
    tokens = pages * page_len
    key_width = kv_heads * HD
    win = key_width // 2
    owner_grp = lax.div(t, share)
    self_part = owner_grp == j

    def tp_peer(d):
        return lax.rem(t + d, tp)

    def tp_src(d):
        return lax.rem(t + (tp - d), tp)

    quarter = group_size // 2

    def head_row(head):
        kv, g = head // group_size, head % group_size
        return (kv // 2) * 2 * group_size + (g % 2) * group_size + (kv % 2) * quarter + g // 2

    barrier = pltpu.get_barrier_semaphore()
    for d in range(1, tp):
        pl.semaphore_signal(barrier, inc=1, device_id=(j, tp_peer(d)), device_id_type=MESH)
    for a in range(1, grp):
        pl.semaphore_signal(
            barrier, inc=1, device_id=(lax.rem(j + a, grp), t), device_id_type=MESH
        )

    pool_pages = kv_v.shape[0]
    step = pool_pages // POOL_CHUNKS
    local = [
        pltpu.make_async_copy(
            kv_hbm.at[0, pl.ds(i * step, step)],
            kv_v.at[pl.ds(i * step, step)],
            local_sem.at[i],
        )
        for i in range(POOL_CHUNKS)
    ]
    w_copy = pltpu.make_async_copy(w_hbm, w_v, local_sem.at[POOL_CHUNKS])
    q_copy = pltpu.make_async_copy(q_hbm.at[0], q_all.at[t], local_sem.at[POOL_CHUNKS + 1])
    nkv_copy = pltpu.make_async_copy(nkv_hbm, nkv_ref, local_sem.at[POOL_CHUNKS + 2])
    len_copy = pltpu.make_async_copy(len_hbm, len_ref, local_sem.at[POOL_CHUNKS + 3])
    pt_copy = pltpu.make_async_copy(pt_hbm, pt_ref, local_sem.at[POOL_CHUNKS + 4])
    q_copy.start()
    nkv_copy.start()
    len_copy.start()
    pt_copy.start()
    for copy in local:
        copy.start()
    w_copy.start()

    q_bd[...] = jnp.zeros_like(q_bd)
    ps[...] = jnp.zeros_like(ps)
    pl.semaphore_wait(barrier, (tp - 1) + (grp - 1))

    q_sends = []
    for d in range(1, tp):
        copy = pltpu.make_async_remote_copy(
            src_ref=q_hbm.at[0],
            dst_ref=q_all.at[t],
            send_sem=q_ssem.at[d],
            recv_sem=q_rsem.at[t],
            device_id=(j, tp_peer(d)),
            device_id_type=MESH,
        )
        copy.start()
        q_sends.append(copy)
    q_copy.wait()
    nkv_copy.wait()

    lane = lax.broadcasted_iota(jnp.int32, (half_slots, LANES), 1)
    low = lane < HD

    kv_own = lax.div(t * own, group_size)
    odd = lax.rem(kv_own, 2)
    lane2 = lax.broadcasted_iota(jnp.int32, (slots, LANES), 1)
    low2 = lane2 < HD

    def kv_tile(base):
        start = pl.multiple_of(base + lax.div(kv_own, 2) * LANES, LANES)
        x = nkv_ref[0, :, pl.ds(start, LANES)].astype(jnp.float32)
        flipped = pltpu.roll(x, HD, 1)
        flip = jnp.broadcast_to(odd, x.shape) == 1
        first = jnp.where(flip, flipped, x)
        return jnp.where(low2, first, pltpu.roll(first, HD, 1))

    new_key = kv_tile(0)
    new_val = kv_tile(key_width)
    q_own = q_all[t].astype(jnp.float32)
    prod = q_own * jnp.concatenate([new_key] * (own // 2), axis=1)
    prod_hi = prod.astype(jnp.bfloat16)
    prod_lo = (prod - prod_hi.astype(jnp.float32)).astype(jnp.bfloat16)
    e_row = lax.broadcasted_iota(jnp.int32, (own * HD, LANES), 0) // HD
    e_col = lax.broadcasted_iota(jnp.int32, (own * HD, LANES), 1) % own
    e_row = (e_row % 2) * (own // 2) + e_row // 2
    spread = jnp.where(e_row == e_col, 1.0, 0.0).astype(jnp.bfloat16)
    self_score = jnp.dot(prod_hi, spread, preferred_element_type=jnp.float32) + jnp.dot(
        prod_lo, spread, preferred_element_type=jnp.float32
    )
    self_score = self_score * (HD**-0.5)

    for d in range(1, tp):
        src = tp_src(d)
        pltpu.make_async_remote_copy(
            src_ref=q_hbm.at[0],
            dst_ref=q_all.at[src],
            send_sem=q_ssem.at[d],
            recv_sem=q_rsem.at[src],
            device_id=(j, src),
            device_id_type=MESH,
        ).wait_recv()
    for src in range(tp):
        rows = q_all[src].astype(jnp.float32) * (HD**-0.5)
        for pair in range(own // 2):
            tile = rows[:, pair * LANES : (pair + 1) * LANES]
            turned = pltpu.roll(tile, HD, 1)
            for side in range(2):
                head = src * own + pair * 2 + side
                kv = head // group_size
                value = tile if side == kv % 2 else turned
                keep = low2 if kv % 2 == 0 else jnp.logical_not(low2)
                value = jnp.where(keep, value, 0.0)
                row = head_row(head)
                q_bd[(kv % half_kv) // 2, pl.ds(row, slots, stride=heads), :] = value

    len_copy.wait()
    pt_copy.wait()
    for copy in local:
        copy.wait()

    col = lax.broadcasted_iota(jnp.int32, (heads, tokens), 1)
    position = ((col // page_len) * tp + t) * page_len + col % page_len
    stat_lane = lax.broadcasted_iota(jnp.int32, (heads, LANES), 1)
    tiles_in_win = win // LANES
    rows_in_win = half_kv * group_size

    def slot_scores(s):
        first = s * heads
        ids = [pt_ref[0, s, i] for i in range(pages)]
        length = len_ref[0, s]

        def block(start):
            return jnp.concatenate(
                [kv_v[ids[i], :, start : start + win] for i in range(pages)], axis=0
            )

        scores = []
        for w in range(2):
            q_w = jnp.concatenate(
                [
                    q_bd[k, pl.ds(first + w * rows_in_win, rows_in_win), :]
                    for k in range(tiles_in_win)
                ],
                axis=1,
            ).astype(jnp.bfloat16)
            scores.append(
                lax.dot_general(
                    q_w,
                    block(w * win),
                    (((1,), (1,)), ((), ())),
                    preferred_element_type=jnp.float32,
                )
            )
        return jnp.concatenate(scores, axis=0), block, length

    def slot_values(scores, block, length):
        valid = position < length
        scores = jnp.where(valid, scores, NEG_BIG)
        top = jnp.max(scores, axis=1, keepdims=True)
        weights = jnp.where(valid, jnp.exp(scores - top), 0.0)
        total = jnp.sum(weights, axis=1, keepdims=True)
        rounded = weights.astype(jnp.bfloat16)
        tiles = []
        for w in range(2):
            o = jnp.dot(
                rounded[w * rows_in_win : (w + 1) * rows_in_win],
                block(key_width + w * win),
                preferred_element_type=jnp.float32,
            )
            for k in range(tiles_in_win):
                base = k * 2 * group_size
                lanes = slice(k * LANES, (k + 1) * LANES)
                a = o[base : base + group_size, lanes]
                b = o[base + group_size : base + 2 * group_size, lanes]
                a = jnp.where(upper, a, pltpu.roll(a, HD, 1))
                b = jnp.where(upper, pltpu.roll(b, HD, 1), b)
                tiles.append(jnp.where(g_low, a, b))
        return tiles, top, total

    g_low = lax.broadcasted_iota(jnp.int32, (group_size, LANES), 1) < HD
    upper = lax.broadcasted_iota(jnp.int32, (group_size, LANES), 0) < quarter
    hs = half_slots
    pairs = own // 2
    span = pairs * hs

    def attend_half(h):
        stats = jnp.zeros((heads, LANES), jnp.float32)
        ahead = 2
        staged = [slot_scores(h * hs + r) for r in range(ahead)]
        for r in range(hs):
            if r + ahead < hs:
                staged.append(slot_scores(h * hs + r + ahead))
            tiles, top, total = slot_values(*staged[r])
            for k in range(kv_heads // 2):
                wbuf[pl.ds(k * group_size * hs + r, group_size, stride=hs), :] = tiles[k]
            stats = jnp.where(stat_lane == r, top, stats)
            stats = jnp.where(stat_lane == r + hs, total, stats)
        for dst in range(tp):
            w_send[h, dst] = wbuf[dst * span : (dst + 1) * span, :].astype(jnp.bfloat16)
            for p in range(2):
                row = head_row(dst * own + p)
                st_send[h, dst, p * pairs : (p + 1) * pairs] = stats[row : row + pairs]

    def exchange(src_of, dst_buf, ssem, rsem, h):
        sends = []
        for d in range(1, tp):
            peer = tp_peer(d)
            copy = pltpu.make_async_remote_copy(
                src_ref=src_of(peer),
                dst_ref=dst_buf.at[h, t],
                send_sem=ssem.at[h, d],
                recv_sem=rsem.at[h, t],
                device_id=(j, peer),
                device_id_type=MESH,
            )
            copy.start()
            sends.append(copy)
        return sends

    def arrive(src_of, dst_buf, ssem, rsem, h):
        for d in range(1, tp):
            src = tp_src(d)
            pltpu.make_async_remote_copy(
                src_ref=src_of(src),
                dst_ref=dst_buf.at[h, src],
                send_sem=ssem.at[h, d],
                recv_sem=rsem.at[h, src],
                device_id=(j, src),
                device_id_type=MESH,
            ).wait_recv()

    def across(x, op):
        shift = own
        while shift < heads:
            x = op(x, pltpu.roll(x, shift, 1))
            shift *= 2
        return x

    def pair_cast(x, base, q):
        a, b = base + q, base + pairs + q
        return jnp.where(
            low,
            jnp.broadcast_to(x[:, a : a + 1], (hs, LANES)),
            jnp.broadcast_to(x[:, b : b + 1], (hs, LANES)),
        )

    def combine_half(h):
        arrive(lambda p: st_send.at[h, p], st_recv, st_ssem, st_rsem, h)
        stacked = jnp.concatenate(
            [st_recv[h, src] for src in range(tp)] * (LANES // heads), axis=0
        )
        turned = jnp.transpose(stacked)
        top, total = turned[:hs], turned[hs : 2 * hs]
        self_h = self_score[h * hs : (h + 1) * hs]
        final = jnp.maximum(across(top, jnp.maximum), self_h)
        scale = jnp.exp(top - final)
        self_w = jnp.exp(self_h - final)
        denominator = across(scale * total, jnp.add) + self_w
        part = scale / denominator
        own_part = self_w / denominator
        value = new_val[h * hs : (h + 1) * hs]
        sums = [pair_cast(own_part, 0, q) * value for q in range(pairs)]
        factors = [[pair_cast(part, src * own, q) for q in range(pairs)] for src in range(tp)]
        arrive(lambda p: w_send.at[h, p], w_recv, w_ssem, w_rsem, h)
        for src in range(tp):
            block = w_recv[h, src].astype(jnp.float32)
            for q in range(pairs):
                sums[q] = sums[q] + factors[src][q] * block[q * hs : (q + 1) * hs]
        attended = jnp.concatenate(sums, axis=1)
        slot_row = lax.broadcasted_iota(jnp.int32, attended.shape, 0) + h * hs
        attended = jnp.where(slot_row < bs_ref[0], attended, 0.0).astype(jnp.bfloat16)
        att_all[h, j] = attended
        sends = []
        for a in range(1, grp):
            copy = pltpu.make_async_remote_copy(
                src_ref=att_all.at[h, j],
                dst_ref=att_all.at[h, j],
                send_sem=a_ssem.at[h, a],
                recv_sem=a_rsem.at[h, j],
                device_id=(lax.rem(j + a, grp), t),
                device_id_type=MESH,
            )
            copy.start()
            sends.append(copy)
        return sends

    width = per * LANES

    def project_half(h):
        for a in range(1, grp):
            src = lax.rem(j + (grp - a), grp)
            pltpu.make_async_remote_copy(
                src_ref=att_all.at[h, src],
                dst_ref=att_all.at[h, src],
                send_sem=a_ssem.at[h, a],
                recv_sem=a_rsem.at[h, src],
                device_id=(src, t),
                device_id_type=MESH,
            ).wait_recv()
        lhs = jnp.concatenate([att_all[h, g] for g in range(grp)], axis=0)
        projected = lax.dot_general(
            lhs, w_v[...], (((1,), (1,)), ((), ())), preferred_element_type=jnp.float32
        )
        for g in range(grp):
            for k in range(share):
                lo, hi = k * width, min((k + 1) * width, cols)
                if lo < hi:
                    ps[h, g, k, :, 0 : hi - lo] = projected[
                        g * hs : (g + 1) * hs, lo:hi
                    ].astype(jnp.bfloat16)
        sends = []
        for a in range(grp):
            dst_g = lax.rem(j + a, grp)
            for k in range(share):
                dst_t = share * j + k
                copy = pltpu.make_async_remote_copy(
                    src_ref=ps.at[h, dst_g, k],
                    dst_ref=rs.at[h, t],
                    send_sem=p_ssem.at[h, a, k],
                    recv_sem=p_rsem.at[h, t],
                    device_id=(dst_g, dst_t),
                    device_id_type=MESH,
                )
                if a == 0:
                    here = dst_t == t

                    @pl.when(jnp.logical_not(here))
                    def _():
                        copy.start()

                    @pl.when(here)
                    def _():
                        rs[h, t] = ps[h, j, k]

                    sends.append((copy, here))
                else:
                    copy.start()
                    sends.append((copy, None))
        return sends

    def sum_half(h):
        for d in range(tp):
            src = tp_src(d)
            copy = pltpu.make_async_remote_copy(
                src_ref=ps.at[h, 0, 0],
                dst_ref=rs.at[h, src],
                send_sem=p_ssem.at[h, 0, 0],
                recv_sem=p_rsem.at[h, src],
                device_id=(owner_grp, src),
                device_id_type=MESH,
            )
            if d == 0:

                @pl.when(jnp.logical_not(self_part))
                def _():
                    copy.wait_recv()

            else:
                copy.wait_recv()
        total = rs[h, 0].astype(jnp.float32)
        for src in range(1, tp):
            total = total + rs[h, src].astype(jnp.float32)
        red[h] = total.astype(jnp.bfloat16)
        sends = exchange(lambda p: red.at[h], og, o_ssem, o_rsem, h)
        og[h, t] = red[h]
        return sends

    sends, p_sends = list(q_sends), []
    for h in range(2):
        attend_half(h)
        sends += exchange(lambda p: st_send.at[h, p], st_recv, st_ssem, st_rsem, h)
        sends += exchange(lambda p: w_send.at[h, p], w_recv, w_ssem, w_rsem, h)
        w_recv[h, t] = w_send[h, t]
        st_recv[h, t] = st_send[h, t]
    w_copy.wait()
    for h in range(2):
        sends += combine_half(h)
    for h in range(2):
        p_sends += project_half(h)
    for h in range(2):
        sends += sum_half(h)
    for h in range(2):
        arrive(lambda p: red.at[h], og, o_ssem, o_rsem, h)
        pieces = []
        for g in range(grp):
            for k in range(share):
                size = min((k + 1) * width, cols) - k * width
                if size > 0:
                    pieces.append(og[h, g * share + k][:, :size].astype(jnp.float32))
        out_ref[0, h * hs : (h + 1) * hs] = jnp.concatenate(pieces, axis=1)
    for copy in sends:
        copy.wait_send()
    for copy, here in p_sends:
        if here is None:
            copy.wait_send()
        else:

            @pl.when(jnp.logical_not(here))
            def _():
                copy.wait_send()


def local(tp, grp, batch_sizes, seq_lens, page_table, queries, kv_pool, new_kv, out_weight):
    out_weight = out_weight.T
    slots, pages = page_table.shape[1:]
    pool_pages, page_len, row_width = kv_pool.shape[1:]
    kv_heads = row_width // (2 * HD)
    own_width = queries.shape[2]
    own = own_width // HD
    heads = own * tp
    cols, rows = out_weight.shape
    share = tp // grp
    tiles = -(-cols // LANES)
    per = -(-tiles // share)
    half = slots // 2
    cfg = (tp, grp, heads, kv_heads, slots, pages, page_len, cols, per, share)
    bf16, f32 = jnp.bfloat16, jnp.float32
    sem = pltpu.SemaphoreType.DMA
    vmem, smem, hbm = (
        pl.BlockSpec(memory_space=pltpu.VMEM),
        pl.BlockSpec(memory_space=pltpu.SMEM),
        pl.BlockSpec(memory_space=pl.ANY),
    )
    return pl.pallas_call(
        functools.partial(fused_kernel, cfg),
        out_shape=jax.ShapeDtypeStruct((1, slots, cols * grp), f32),
        in_specs=[smem] + [hbm] * 6,
        out_specs=vmem,
        scratch_shapes=[
            pltpu.SMEM(seq_lens.shape, jnp.int32),
            pltpu.SMEM(page_table.shape, jnp.int32),
            pltpu.VMEM(new_kv.shape, bf16),
            pltpu.VMEM((pool_pages, page_len, row_width), bf16),
            pltpu.VMEM((cols, rows), bf16),
            pltpu.VMEM((tp, slots, own_width), bf16),
            pltpu.VMEM((kv_heads * HD // (2 * LANES), slots * heads, LANES), f32),
            pltpu.VMEM((heads * half // 2, LANES), f32),
            pltpu.VMEM((2, tp, own // 2 * half, LANES), bf16),
            pltpu.VMEM((2, tp, own, LANES), f32),
            pltpu.VMEM((2, tp, own // 2 * half, LANES), bf16),
            pltpu.VMEM((2, tp, own, LANES), f32),
            pltpu.VMEM((2, grp, half, own_width), bf16),
            pltpu.VMEM((2, grp, share, half, per * LANES), bf16),
            pltpu.VMEM((2, tp, half, per * LANES), bf16),
            pltpu.VMEM((2, half, per * LANES), bf16),
            pltpu.VMEM((2, tp, half, per * LANES), bf16),
            sem((POOL_CHUNKS + 5,)),
            sem((tp,)),
            sem((tp,)),
            sem((2, tp)),
            sem((2, tp)),
            sem((2, tp)),
            sem((2, tp)),
            sem((2, grp)),
            sem((2, grp)),
            sem((2, grp, share)),
            sem((2, tp)),
            sem((2, tp)),
            sem((2, tp)),
        ],
        compiler_params=pltpu.CompilerParams(
            collective_id=0, has_side_effects=True, vmem_limit_bytes=60 * 1024 * 1024
        ),
        name="fused_decode",
    )(batch_sizes, seq_lens, page_table, queries, kv_pool, new_kv, out_weight)


def solution(mesh):
    return jax.shard_map(
        functools.partial(local, mesh.shape["tp"], mesh.shape["grp"]),
        mesh=mesh,
        in_specs=(
            P("grp"),
            P("grp", None),
            P("grp", None, "tp"),
            P("grp", None, "tp"),
            P("grp", "tp", None, None),
            P("grp", None, None),
            P("tp", "grp"),
        ),
        out_specs=P("grp", None, None),
        check_vma=False,
    )
```
